128 devices in a mesh: frame: 4 (over z_lo, core), lat: 4 (over y), lon: 8 (over z_hi, x).
Axes of the slice: x: 4, y: 4, z: 4 (z_hi: 2, z_lo: 2; z = z_hi * 2 + z_lo), core: 2. Of those that a mesh axis runs over, the one named last changes fastest.
Arguments:
- frames_in: bfloat16 [16, 32, 256, 512], P('frame', 'lat', 'lon'), may hold values from -6 to 6
- grad_out: bfloat16 [16, 32, 256, 512], P('frame', 'lat', 'lon'), may hold values from -6 to 6
- kernel: bfloat16 [49, 512], replicated, may hold values from -0.875 to 0.875
- w_qkv: bfloat16 [512, 1536], replicated, may hold values from -0.25 to 0.25
- w_out: bfloat16 [512, 512], replicated, may hold values from -0.25 to 0.25
Outputs:
- grad_input: bfloat16 [16, 32, 256, 512], P('frame', 'lat', 'lon')
- grad_proj: float32 [512, 2048], P(('frame', 'lat', 'lon'))
- grad_kernel: float32 [49, 512], replicated
The draws below stay inside these ranges and needn't reach their ends.
All inputs are finite; a program needn't handle non-finite values.
Results may differ from the reference program's by a relative error of at most 0.0098.
Values may be sent and summed in bfloat16 or wider, within the bound.
No kernel may reach another device: no remote copies, remote signals or barrier semaphores. Data moves between devices by JAX's collectives and lax.ppermute only.
A program may use at most 128 MiB of HBM per device.

```python
import math
import jax
import jax.numpy as jnp
from jax import lax

CHANNELS = 512
HEADS = 4
FRAMES = 16
KSIZE = 7
TAPS = 49
GRID_LAT = 32
GRID_LON = 256


def levels(key, dims, shards, smallest, top_value):
    loudness, own = 1.0, jax.random.fold_in(key, 6)
    for dim, shards_of in shards:
        draws = jnp.exp(jax.random.uniform(jax.random.fold_in(own, dim), (shards_of,), jnp.float32, smallest / len(shards), top_value / len(shards)))
        loudness = loudness * jnp.repeat(draws, dims[dim] // shards_of).reshape([-1 if axis == dim else 1 for axis in range(len(dims))])
    return loudness


def normal_values(own_key, shape, scale, reach, cuts=(), dtype=jnp.bfloat16):
    entries = jax.random.normal(own_key, shape, jnp.float32) * scale
    if len(cuts) > 0:
        entries = levels(own_key, shape, cuts, -0.22, 0.18) * entries
    return jnp.clip(entries, min=-reach, max=reach).astype(dtype)


def setup_inputs(seed: int = 0) -> dict:
    key_of = jax.random.split(jax.random.key(seed), 6)
    return {
        "frames_in": normal_values(key_of[0], (FRAMES, GRID_LAT, GRID_LON, CHANNELS), 1.0, 6.0, ((0, 4), (1, 4), (2, 8))),
        "grad_out": normal_values(key_of[1], (FRAMES, GRID_LAT, GRID_LON, CHANNELS), 1.0, 6.0, ((0, 4), (1, 4), (2, 8))),
        "kernel": normal_values(key_of[2], (TAPS, CHANNELS), TAPS ** -0.5, 0.875),
        "w_qkv": normal_values(key_of[3], (CHANNELS, 3 * CHANNELS), CHANNELS ** -0.5, 0.25),
        "w_out": normal_values(key_of[4], (CHANNELS, CHANNELS), CHANNELS ** -0.5, 0.25),
    }


def conv_taps(padded, kernel, rows, cols, flipped):
    side = math.isqrt(kernel.shape[0])
    total = jnp.zeros((padded.shape[0], rows, cols, padded.shape[3]), jnp.float32)
    for row_tap in range(side):
        for col_tap in range(side):
            weight = kernel[row_tap * side + col_tap].astype(jnp.float32)
            if flipped:
                start_row = side - 1 - row_tap
                start_col = side - 1 - col_tap
            else:
                start_row = row_tap
                start_col = col_tap
            window = padded[:, start_row:start_row + rows, start_col:start_col + cols, :]
            total = total + weight * window.astype(jnp.float32)
    return total

def tap_products(padded, grad_mixed, side):
    rows = grad_mixed.shape[1]
    cols = grad_mixed.shape[2]
    grad_wide = grad_mixed.astype(jnp.float32)
    terms = []
    for row_tap in range(side):
        for col_tap in range(side):
            window = padded[:, row_tap:row_tap + rows, col_tap:col_tap + cols, :].astype(jnp.float32)
            terms.append(lax.optimization_barrier(jnp.sum(window * grad_wide, axis=(0, 1, 2))))
    return jnp.stack(terms, axis=0)

def attend(projected, grad_rows, w_out, heads):
    frames, count, triple = projected.shape
    width = triple // 3
    depth = width // heads
    scale = depth ** (-0.5)
    queries = projected[:, :, :width].reshape(frames, count, heads, depth).astype(jnp.float32)
    key_rows = projected[:, :, width:2 * width].reshape(frames, count, heads, depth).astype(jnp.float32)
    value_rows = projected[:, :, 2 * width:].reshape(frames, count, heads, depth).astype(jnp.float32)
    scores = jnp.einsum('ithd,jthd->ijht', queries, key_rows) * scale
    raised = jnp.exp(scores)
    probs = raised / lax.optimization_barrier(jnp.sum(raised, axis=1, keepdims=True))
    probs_low = probs.astype(jnp.bfloat16)
    attended = jnp.einsum('ijht,jthd->ithd', probs_low.astype(jnp.float32), value_rows).astype(jnp.bfloat16)
    grad_flat = grad_rows.reshape(frames * count, width)
    grad_att = lax.dot_general(grad_flat, w_out, (((1,), (1,)), ((), ())), preferred_element_type=jnp.float32)
    grad_att = grad_att.astype(jnp.bfloat16).reshape(frames, count, heads, depth).astype(jnp.float32)
    grad_probs = jnp.einsum('ithd,jthd->ijht', grad_att, value_rows)
    inner = lax.optimization_barrier(jnp.sum(probs * grad_probs, axis=1, keepdims=True))
    grad_scores = (probs * (grad_probs - inner) * scale).astype(jnp.bfloat16).astype(jnp.float32)
    grad_query = jnp.einsum('ijht,jthd->ithd', grad_scores, key_rows).astype(jnp.bfloat16)
    grad_key = jnp.einsum('ijht,ithd->jthd', grad_scores, queries).astype(jnp.bfloat16)
    grad_value = jnp.einsum('ijht,ithd->jthd', probs_low.astype(jnp.float32), grad_att).astype(jnp.bfloat16)
    stacked = jnp.concatenate([grad_query.reshape(frames, count, width), grad_key.reshape(frames, count, width), grad_value.reshape(frames, count, width)], axis=2)
    return (stacked, attended.reshape(frames, count, width))

def reference(frames_in, grad_out, kernel, w_qkv, w_out):
    half = KSIZE // 2
    pad_spec = ((0, 0), (half, half), (half, half), (0, 0))
    width = CHANNELS

    def forward_frame(frame):
        padded = jnp.pad(frame[None], pad_spec)
        return conv_taps(padded, kernel, GRID_LAT, GRID_LON, False).astype(jnp.bfloat16)[0]
    mixed = lax.map(forward_frame, frames_in)
    mixed_lat = jnp.transpose(mixed, (1, 0, 2, 3))
    grad_lat = jnp.transpose(grad_out, (1, 0, 2, 3))

    def row_step(carry, item):
        mixed_row, grad_row = item
        mixed_flat = mixed_row.reshape(-1, width)
        projected = jnp.dot(mixed_flat, w_qkv, preferred_element_type=jnp.float32).astype(jnp.bfloat16)
        projected = projected.reshape(FRAMES, GRID_LON, 3 * width)
        stacked, attended = attend(projected, grad_row, w_out, HEADS)
        flat_grad = stacked.reshape(-1, 3 * width)
        grad_mix = lax.dot_general(flat_grad, w_qkv, (((1,), (1,)), ((), ())), preferred_element_type=jnp.float32)
        grad_mix = grad_mix.astype(jnp.bfloat16).reshape(FRAMES, GRID_LON, width)
        qkv_term = lax.dot_general(mixed_flat, flat_grad, (((0,), (0,)), ((), ())), preferred_element_type=jnp.float32)
        out_term = lax.dot_general(attended.reshape(-1, width), grad_row.reshape(-1, width), (((0,), (0,)), ((), ())), preferred_element_type=jnp.float32)
        return ((carry[0] + qkv_term, carry[1] + out_term), grad_mix)
    start = (jnp.zeros((width, 3 * width), jnp.float32), jnp.zeros((width, width), jnp.float32))
    sums, grad_mix_lat = lax.scan(row_step, start, (mixed_lat, grad_lat))
    grad_mixed = jnp.transpose(grad_mix_lat, (1, 0, 2, 3))

    def frame_step(carry, item):
        frame, grad_frame, grad_mix = item
        padded = jnp.pad(frame[None], pad_spec)
        grad_pad = jnp.pad(grad_mix[None], pad_spec)
        adjoint = conv_taps(grad_pad, kernel, GRID_LAT, GRID_LON, True)[0]
        grad_in = (grad_frame.astype(jnp.float32) + adjoint).astype(jnp.bfloat16)
        return (carry + tap_products(padded, grad_mix[None], KSIZE), grad_in)
    kernel_total, grad_input = lax.scan(frame_step, jnp.zeros((TAPS, width), jnp.float32), (frames_in, grad_out, grad_mixed))
    scale = (FRAMES * GRID_LAT * GRID_LON) ** (-0.5)
    grad_proj = jnp.concatenate([sums[0], sums[1]], axis=1) * scale
    return (grad_input, grad_proj, kernel_total * scale)
```

```python
import math

import jax
import jax.numpy as jnp
from jax import lax
from jax.experimental import pallas as pl
from jax.experimental.pallas import tpu as pltpu
from jax.sharding import PartitionSpec as P

HEADS = 4
LANES = 128
EDGE = 8
F32 = jnp.float32
BF16 = jnp.bfloat16


def halo(block, half):
    rows, cols = block.shape[1], block.shape[2]
    lats, lons = lax.axis_size("lat"), lax.axis_size("lon")
    row_part = {
        -1: lax.slice_in_dim(block, rows - half, rows, axis=1),
        0: block,
        1: lax.slice_in_dim(block, 0, half, axis=1),
    }
    parts = {}
    for dy, dx in ((-1, 0), (1, 0), (0, -1), (0, 1), (-1, -1), (-1, 1), (1, -1), (1, 1)):
        piece = row_part[dy]
        if dx == -1:
            piece = lax.slice_in_dim(piece, cols - half, cols, axis=2)
        elif dx == 1:
            piece = lax.slice_in_dim(piece, 0, half, axis=2)
        pairs = []
        for y in range(lats):
            for x in range(lons):
                from_y, from_x = y + dy, x + dx
                if 0 <= from_y < lats and 0 <= from_x < lons:
                    pairs.append((from_y * lons + from_x, y * lons + x))
        parts[(dy, dx)] = lax.ppermute(piece, ("lat", "lon"), pairs)
    return [
        parts[at]
        for at in ((-1, 0), (1, 0), (0, -1), (0, 1), (-1, -1), (-1, 1), (1, -1), (1, 1))
    ]


def fill_padded(pad, c, n, s, w, e, nw, ne, sw, se):
    rows, cols = c.shape[1], c.shape[2]
    half = n.shape[1]
    low, high = half + rows, EDGE + cols
    pad[half:low, EDGE:high, :] = c[0].astype(F32)
    pad[0:half, EDGE:high, :] = n[0].astype(F32)
    pad[low : low + half, EDGE:high, :] = s[0].astype(F32)
    pad[half:low, EDGE - half : EDGE, :] = w[0].astype(F32)
    pad[half:low, high : high + half, :] = e[0].astype(F32)
    pad[0:half, EDGE - half : EDGE, :] = nw[0].astype(F32)
    pad[0:half, high : high + half, :] = ne[0].astype(F32)
    pad[low : low + half, EDGE - half : EDGE, :] = sw[0].astype(F32)
    pad[low : low + half, high : high + half, :] = se[0].astype(F32)


def conv_body(flipped, residual, c, n, s, w, e, nw, ne, sw, se, k, *rest):
    if residual:
        base, out, pad, taps = rest
    else:
        out, pad, taps = rest
    rows, cols = c.shape[1], c.shape[2]
    side = 2 * n.shape[1] + 1
    fill_padded(pad, c, n, s, w, e, nw, ne, sw, se)
    taps[0 : side * side, :] = k[...].astype(F32)
    start = EDGE - n.shape[1]
    for col in range(0, cols, 16):
        sums = [[jnp.zeros((8, LANES), F32) for _ in range(2)] for _ in range(rows)]
        for col_tap in range(side):
            weights = []
            for row_tap in range(side):
                at = row_tap * side + col_tap
                if flipped:
                    at = side * side - 1 - at
                weights.append(jnp.broadcast_to(taps[at : at + 1, :], (8, LANES)))
            for y in range(rows + side - 1):
                for part in range(2):
                    first = start + col + 8 * part + col_tap
                    value = pad[y, first : first + 8, :]
                    for row_tap in range(side):
                        if 0 <= y - row_tap < rows:
                            sums[y - row_tap][part] += weights[row_tap] * value
        for y in range(rows):
            total = jnp.concatenate(sums[y], axis=0)
            if residual:
                total = total + base[0, y, col : col + 16, :].astype(F32)
            out[0, y, col : col + 16, :] = total.astype(BF16)


def tile_specs(block, pieces, index):
    return [pl.BlockSpec((1,) + a.shape[1:3] + (LANES,), index) for a in (block, *pieces)]


def convolve(block, pieces, kernel, flipped, base=None):
    frames, rows, cols, width = block.shape
    taps = kernel.shape[0]
    half = pieces[0].shape[1]

    def index(f, c):
        return (f, 0, 0, c)

    specs = tile_specs(block, pieces, index)
    specs.append(pl.BlockSpec((taps, LANES), lambda f, c: (0, c)))
    operands = [block, *pieces, kernel]
    if base is not None:
        specs.append(pl.BlockSpec((1, rows, cols, LANES), index))
        operands.append(base)

    def body(*refs):
        conv_body(flipped, base is not None, *refs)

    return pl.pallas_call(
        body,
        name="conv_adjoint" if flipped else "conv_forward",
        grid=(frames, width // LANES),
        in_specs=specs,
        out_specs=pl.BlockSpec((1, rows, cols, LANES), index),
        out_shape=jax.ShapeDtypeStruct(block.shape, BF16),
        scratch_shapes=[
            pltpu.VMEM((rows + 2 * half, cols + 2 * EDGE, LANES), F32),
            pltpu.VMEM((-(-taps // 8) * 8, LANES), F32),
        ],
        cost_estimate=pl.CostEstimate(
            flops=2 * taps * block.size, bytes_accessed=6 * block.size, transcendentals=0
        ),
    )(*operands)


def taps_body(c, n, s, w, e, nw, ne, sw, se, g, out, pad, wide, total):
    rows, cols = c.shape[1], c.shape[2]
    side = 2 * n.shape[1] + 1
    frame = pl.program_id(1)

    @pl.when(frame == 0)
    def _():
        total[...] = jnp.zeros_like(total)

    fill_padded(pad, c, n, s, w, e, nw, ne, sw, se)
    wide[...] = g[0].astype(F32)
    start = EDGE - n.shape[1]
    for col in range(0, cols, 16):
        grads = [
            [wide[y, col + 8 * part : col + 8 * part + 8, :] for part in range(2)]
            for y in range(rows)
        ]
        for col_tap in range(side):
            sums = [total[r * side + col_tap] for r in range(side)]
            for y in range(rows + side - 1):
                for part in range(2):
                    first = start + col + 8 * part + col_tap
                    value = pad[y, first : first + 8, :]
                    for row_tap in range(side):
                        if 0 <= y - row_tap < rows:
                            sums[row_tap] += value * grads[y - row_tap][part]
            for r in range(side):
                total[r * side + col_tap] = sums[r]

    @pl.when(frame == pl.num_programs(1) - 1)
    def _():
        out[...] = jnp.sum(total[...], axis=1)


def tap_products(block, pieces, grad_mixed):
    frames, rows, cols, width = block.shape
    half = pieces[0].shape[1]
    taps = (2 * half + 1) ** 2

    def index(c, f):
        return (f, 0, 0, c)

    return pl.pallas_call(
        taps_body,
        name="tap_products",
        grid=(width // LANES, frames),
        in_specs=tile_specs(block, pieces, index)
        + [pl.BlockSpec((1, rows, cols, LANES), index)],
        out_specs=pl.BlockSpec((taps, LANES), lambda c, f: (0, c)),
        out_shape=jax.ShapeDtypeStruct((taps, width), F32),
        scratch_shapes=[
            pltpu.VMEM((rows + 2 * half, cols + 2 * EDGE, LANES), F32),
            pltpu.VMEM((rows, cols, LANES), F32),
            pltpu.VMEM((taps, 8, LANES), F32),
        ],
        cost_estimate=pl.CostEstimate(
            flops=2 * taps * block.size, bytes_accessed=6 * block.size, transcendentals=0
        ),
    )(block, *pieces, grad_mixed)


def dot(a, b, over):
    return lax.dot_general(a, b, ((over[:1], over[1:]), ((), ())), preferred_element_type=F32)


def attend_body(x, g, w_qkv, w_out, token_grad, stacked, attended):
    frames, cells, width = x.shape
    rows = frames * cells
    depth = width // HEADS
    scale = depth ** (-0.5)
    mixed = x[...].reshape(rows, width)
    grads = g[...].reshape(rows, width)
    projected = dot(mixed, w_qkv[...], (1, 0)).astype(BF16)
    grad_att = dot(grads, w_out[...], (1, 1)).astype(BF16)
    at_row = lax.broadcasted_iota(jnp.int32, (rows, rows), 0)
    at_col = lax.broadcasted_iota(jnp.int32, (rows, rows), 1)
    same = lax.rem(at_row, cells) == lax.rem(at_col, cells)
    attended_parts, query_parts, key_parts, value_parts = [], [], [], []
    for head in range(HEADS):
        at = head * depth
        query = projected[:, at : at + depth]
        key = projected[:, width + at : width + at + depth]
        value = projected[:, 2 * width + at : 2 * width + at + depth]
        grad_a = grad_att[:, at : at + depth]
        scores = dot(key, query, (1, 1)) * scale
        raised = jnp.exp(jnp.where(same, scores, -jnp.inf))
        probs = raised * (1.0 / jnp.sum(raised, axis=0, keepdims=True))
        low = probs.astype(BF16)
        attended_parts.append(dot(low, value, (0, 0)).astype(BF16))
        grad_probs = dot(value, grad_a, (1, 1))
        inner = jnp.sum(probs * grad_probs, axis=0, keepdims=True)
        grad_scores = (probs * (grad_probs - inner) * scale).astype(BF16)
        query_parts.append(dot(grad_scores, key, (0, 0)).astype(BF16))
        key_parts.append(dot(grad_scores, query, (1, 0)).astype(BF16))
        value_parts.append(dot(low, grad_a, (1, 0)).astype(BF16))
    attended[...] = jnp.concatenate(attended_parts, axis=1).reshape(frames, cells, width)
    grad_qkv = jnp.concatenate(query_parts + key_parts + value_parts, axis=1)
    stacked[...] = grad_qkv.reshape(frames, cells, 3 * width)
    back = dot(grad_qkv, w_qkv[...], (1, 1)).astype(BF16)
    token_grad[...] = back.reshape(frames, cells, width)


def attend(mixed, grads, w_qkv, w_out):
    frames, cells, width = mixed.shape
    group = 16

    def rows_of(size):
        return pl.BlockSpec((frames, group, size), lambda i: (0, i, 0))

    tokens = frames * cells
    return pl.pallas_call(
        attend_body,
        name="attend",
        grid=(cells // group,),
        in_specs=[
            rows_of(width),
            rows_of(width),
            pl.BlockSpec(w_qkv.shape, lambda i: (0, 0)),
            pl.BlockSpec(w_out.shape, lambda i: (0, 0)),
        ],
        out_specs=[rows_of(width), rows_of(3 * width), rows_of(width)],
        out_shape=[
            jax.ShapeDtypeStruct((frames, cells, width), BF16),
            jax.ShapeDtypeStruct((frames, cells, 3 * width), BF16),
            jax.ShapeDtypeStruct((frames, cells, width), BF16),
        ],
        cost_estimate=pl.CostEstimate(
            flops=2 * tokens * width * width * 8,
            bytes_accessed=18 * tokens * width,
            transcendentals=tokens * 16 * HEADS,
        ),
    )(mixed, grads, w_qkv, w_out)


def weight_body(mine, x, stacked, attended, g, out):
    rows = out.shape[2]
    width = g.shape[1]
    first = x[...]
    out[0, 0, :, 0 : 3 * width] = dot(first, stacked[...], (0, 0))
    out[0, 0, :, 3 * width :] = dot(attended[...], g[...], (0, 0))


def weight_terms(core, mixed, stacked, attended, grads):
    tokens, width = mixed.shape
    quarter = width // 4
    grid_spec = pltpu.PrefetchScalarGridSpec(
        num_scalar_prefetch=1,
        grid=(4,),
        in_specs=[
            pl.BlockSpec((tokens, quarter), lambda i, c: (0, i)),
            pl.BlockSpec((tokens, 3 * width), lambda i, c: (0, 0)),
            pl.BlockSpec((tokens, quarter), lambda i, c: (0, i)),
            pl.BlockSpec((tokens, width), lambda i, c: (0, 0)),
        ],
        out_specs=pl.BlockSpec(
            (1, 1, quarter, 4 * width), lambda i, c: (lax.rem(i + c[0], 2), i // 2, 0, 0)
        ),
    )
    return pl.pallas_call(
        weight_body,
        name="weight_terms",
        grid_spec=grid_spec,
        out_shape=jax.ShapeDtypeStruct((2, 2, quarter, 4 * width), F32),
        cost_estimate=pl.CostEstimate(
            flops=2 * tokens * width * width * 4,
            bytes_accessed=12 * tokens * width + 16 * width * width,
            transcendentals=0,
        ),
    )(core, mixed, stacked, attended, grads)


def on_device(frames_in, grad_out, kernel, w_qkv, w_out):
    local_frames, tile_lat, tile_lon, width = frames_in.shape
    half = math.isqrt(kernel.shape[0]) // 2
    frame_index = lax.axis_index("frame")
    core = lax.rem(frame_index, 2)
    clip_groups = lax.axis_size("frame")
    cell_groups = lax.axis_size("lat") * lax.axis_size("lon")

    pieces = halo(frames_in, half)
    spread_grad = lax.all_to_all(grad_out, "frame", split_axis=1, concat_axis=0, tiled=True)
    mixed = convolve(frames_in, pieces, kernel, False)
    spread_mixed = lax.all_to_all(mixed, "frame", split_axis=1, concat_axis=0, tiled=True)
    frames = spread_mixed.shape[0]
    mixed_rows = spread_mixed.reshape(frames, -1, width)
    grad_rows = spread_grad.reshape(frames, -1, width)
    token_grad, stacked, attended = attend(mixed_rows, grad_rows, w_qkv, w_out)
    token_grad = token_grad.reshape(spread_mixed.shape)
    grad_mixed = lax.all_to_all(token_grad, "frame", split_axis=0, concat_axis=1, tiled=True)

    terms = weight_terms(
        core.reshape(1).astype(jnp.int32),
        mixed_rows.reshape(-1, width),
        stacked.reshape(-1, 3 * width),
        attended.reshape(-1, width),
        grad_rows.reshape(-1, width),
    )
    swap = [(i, i ^ 1) for i in range(clip_groups)]
    chip_sum = (terms[0] + lax.ppermute(terms[1], "frame", swap)).astype(BF16)
    chip_sum = chip_sum.reshape(2, cell_groups, -1, 4 * width)
    arrived = lax.all_to_all(chip_sum, ("lat", "lon"), split_axis=1, concat_axis=1, tiled=True)
    cell_sum = jnp.sum(arrived.astype(F32), axis=1)
    upper = frame_index // 2
    keep = lax.dynamic_index_in_dim(cell_sum, upper, axis=0, keepdims=False)
    give = lax.dynamic_index_in_dim(cell_sum, 1 - upper, axis=0, keepdims=False)
    across = [(i, i ^ 2) for i in range(clip_groups)]
    proj_sum = keep + lax.ppermute(give, "frame", across)

    grad_pieces = halo(grad_mixed, half)
    kernel_part = tap_products(frames_in, pieces, grad_mixed)
    grad_input = convolve(grad_mixed, grad_pieces, kernel, True, grad_out)

    everyone = ("frame", "lat", "lon")
    count = clip_groups * cell_groups
    spread = kernel_part.reshape(count, -1)
    mine = lax.all_to_all(spread, everyone, split_axis=0, concat_axis=0, tiled=True)
    mine = jnp.sum(mine, axis=0, keepdims=True)
    mine = jnp.broadcast_to(mine, spread.shape)
    kernel_sum = lax.all_to_all(mine, everyone, split_axis=0, concat_axis=0, tiled=True)
    kernel_sum = kernel_sum.reshape(kernel_part.shape)

    scale = (local_frames * clip_groups * tile_lat * tile_lon * cell_groups) ** (-0.5)
    return (grad_input, proj_sum * scale, kernel_sum * scale)


def solution(mesh):
    in_specs = (P("frame", "lat", "lon", None), P("frame", "lat", "lon", None), P(), P(), P())
    out_specs = (P("frame", "lat", "lon", None), P(("frame", "lat", "lon"), None), P())
    return jax.shard_map(
        on_device, mesh=mesh, in_specs=in_specs, out_specs=out_specs, check_vma=False
    )
```

```python
import math

import jax
import jax.numpy as jnp
from jax import lax
from jax.experimental import pallas as pl
from jax.experimental.pallas import tpu as pltpu
from jax.sharding import PartitionSpec as P


HEADS = 4
LANES = 128
EDGE = 8
F32 = jnp.float32
BF16 = jnp.bfloat16


def shift(piece, axis, step):
    count = lax.axis_size(axis)
    pairs = [(i, i + step) for i in range(count) if 0 <= i + step < count]
    return lax.ppermute(piece, axis, pairs)


def rows_around(top, bottom):
    above = shift(bottom, "lat", 1)
    below = shift(top, "lat", -1)
    return above, below


def columns_around(left, right):
    before = shift(right, "lon", 1)
    after = shift(left, "lon", -1)
    return before, after


def ends(parts, half):
    cols = parts[0].shape[2]
    left = jnp.concatenate([a[:, :, :half] for a in parts], axis=1)
    right = jnp.concatenate([a[:, :, cols - half :] for a in parts], axis=1)
    return left, right


def call(body, grid, ins, outs, scratch=(), flops=0, arrays=None, prefetch=0):
    moved = sum(a.size * a.dtype.itemsize for a, _, _ in ins)
    moved += sum(math.prod(o[0]) * jnp.dtype(o[1]).itemsize for o in outs)
    results = pl.pallas_call(
        body,
        grid_spec=pltpu.PrefetchScalarGridSpec(
            num_scalar_prefetch=prefetch,
            grid=grid,
            in_specs=[pl.BlockSpec(block, index) for _, block, index in ins],
            out_specs=[pl.BlockSpec(block, index) for _, _, block, index in outs],
            scratch_shapes=scratch,
        ),
        out_shape=[jax.ShapeDtypeStruct(o[0], o[1]) for o in outs],
        cost_estimate=pl.CostEstimate(flops=flops, bytes_accessed=moved, transcendentals=0),
    )(*(arrays or ()), *[a for a, _, _ in ins])
    return results[0] if len(outs) == 1 else results


INNER, OUTER = (8, 16), (0, 24)


def put(dst, y, col, value):
    for piece, at in enumerate(col):
        dst[y, at : at + 8, :] = value[8 * piece : 8 * piece + 8, :]


def fill_plain(pad, f, c, n, s, half):
    rows, cols = c.shape[1], c.shape[2]
    pad[half : half + rows, EDGE : EDGE + cols, :] = c[f].astype(F32)
    pad[0:half, EDGE : EDGE + cols, :] = n[f].astype(F32)
    pad[half + rows : rows + 2 * half, EDGE : EDGE + cols, :] = s[f].astype(F32)


def fill_sides(pad, f, w, e, half, cols):
    pad[:, EDGE - half : EDGE, :] = w[f].astype(F32)
    pad[:, EDGE + cols : EDGE + cols + half, :] = e[f].astype(F32)


def chunked_row(pad, y, inner, outer):
    put(pad, y, [EDGE + at for at in INNER], inner.astype(F32))
    put(pad, y, [EDGE + at for at in OUTER], outer.astype(F32))


def fill_chunked(pad, f, inner, outer, n, s, half):
    size = inner.shape[2]
    rows = inner.shape[0] * size
    for y in range(rows):
        at = (y // size, f, y % size)
        chunked_row(pad, half + y, inner[at], outer[at])
    for y in range(half):
        chunked_row(pad, y, n[f, y, 0:16, :], n[f, y, 16:32, :])
        chunked_row(pad, half + rows + y, s[f, y, 0:16, :], s[f, y, 16:32, :])


def each_frame(frames, step):
    lax.fori_loop(0, frames, lambda f, done: (step(f), done)[1], 0)


def conv_sums(pad, taps, rows, half, columns, flipped):
    side = 2 * half + 1
    sums = [[jnp.zeros((8, LANES), F32) for _ in columns] for _ in range(rows)]
    for col_tap in range(side):
        weights = []
        for row_tap in range(side):
            at = row_tap * side + col_tap
            if flipped:
                at = side * side - 1 - at
            weights.append(jnp.broadcast_to(taps[at : at + 1, :], (8, LANES)))
        for y in range(rows + side - 1):
            for part, col in enumerate(columns):
                first = EDGE - half + col + col_tap
                value = pad[y, first : first + 8, :]
                for row_tap in range(side):
                    if 0 <= y - row_tap < rows:
                        sums[y - row_tap][part] += weights[row_tap] * value
    return [jnp.concatenate(pair, axis=0) for pair in sums]


def wide_tap(kernel):
    return (kernel, (kernel.shape[0], LANES), lambda c: (0, c))


def tile4(a):
    return (a, a.shape[:3] + (LANES,), lambda c: (0, 0, 0, c))


def tile5(a):
    return (a, a.shape[:4] + (LANES,), lambda c: (0, 0, 0, 0, c))


def conv_scratch(rows, cols, half, taps):
    return [
        pltpu.VMEM((rows + 2 * half, cols + 2 * EDGE, LANES), F32),
        pltpu.VMEM((-(-taps // 8) * 8, LANES), F32),
    ]


def conv_forward(block, above, below, sides, kernel, groups):
    frames, rows, cols, width = block.shape
    count = kernel.shape[0]
    half = above.shape[1]
    size = rows // groups
    columns = OUTER if sides else INNER

    def body(c, n, s, *rest):
        if sides:
            w, e, k, out, pad, taps = rest
        else:
            k, out, pad, taps = rest
        taps[0:count, :] = k[...].astype(F32)

        def one(f):
            fill_plain(pad, f, c, n, s, half)
            if sides:
                fill_sides(pad, f, w, e, half, cols)
            for y, total in enumerate(conv_sums(pad, taps, rows, half, columns, False)):
                out[y // size, f, y % size] = total.astype(BF16)

        each_frame(frames, one)

    shape = (groups, frames, size, 16, width)
    return call(
        body,
        (width // LANES,),
        [tile4(a) for a in (block, above, below, *sides)] + [wide_tap(kernel)],
        [(shape, BF16) + tile5(jax.ShapeDtypeStruct(shape, BF16))[1:]],
        conv_scratch(rows, cols, half, count),
        flops=count * block.size,
    )


def conv_adjoint(inner, outer, above, below, sides, kernel, base, before):
    frames, rows, cols, width = base.shape
    count = kernel.shape[0]
    half = above.shape[1]
    columns = OUTER if sides else INNER

    def body(i, o, n, s, g, *rest):
        if sides:
            w, e, b, k, out, pad, taps = rest
        else:
            k, out, pad, taps = rest
        taps[0:count, :] = k[...].astype(F32)

        def one(f):
            fill_chunked(pad, f, i, o, n, s, half)
            if sides:
                fill_sides(pad, f, w, e, half, cols)
            for y, total in enumerate(conv_sums(pad, taps, rows, half, columns, True)):
                grads = g[f, y].astype(F32)
                grads = [grads[at : at + 8, :] for at in columns]
                total = total + jnp.concatenate(grads, axis=0)
                if sides:
                    pieces = [total[:8], b[f, y].astype(F32), total[8:]]
                    total = jnp.concatenate(pieces, axis=0)
                out[f, y] = total.astype(BF16)

        each_frame(frames, one)

    shape = base.shape if sides else (frames, rows, 16, width)
    extra = [tile4(a) for a in (*sides, before)] if sides else []
    return call(
        body,
        (width // LANES,),
        [tile5(inner), tile5(outer), tile4(above), tile4(below), tile4(base)]
        + extra
        + [wide_tap(kernel)],
        [(shape, BF16) + tile4(jax.ShapeDtypeStruct(shape, BF16))[1:]],
        conv_scratch(rows, cols, half, count),
        flops=count * base.size,
    )


def tap_products(block, pieces, inner, outer, out_rows):
    frames, rows, cols, width = block.shape
    half = pieces[0].shape[1]
    side = 2 * half + 1
    size = inner.shape[2]

    def body(c, n, s, w, e, i, o, out, pad, wide, total):
        total[...] = jnp.zeros_like(total)

        def one(f):
            fill_plain(pad, f, c, n, s, half)
            fill_sides(pad, f, w, e, half, cols)
            for y in range(rows):
                at = (y // size, f, y % size)
                put(wide, y, INNER, i[at].astype(F32))
                put(wide, y, OUTER, o[at].astype(F32))
            for col in range(0, cols, 16):
                grads = [
                    [wide[y, col + 8 * part : col + 8 * part + 8, :] for part in range(2)]
                    for y in range(rows)
                ]
                for col_tap in range(side):
                    sums = [total[r * side + col_tap] for r in range(side)]
                    for y in range(rows + side - 1):
                        for part in range(2):
                            first = EDGE - half + col + 8 * part + col_tap
                            value = pad[y, first : first + 8, :]
                            for row_tap in range(side):
                                if 0 <= y - row_tap < rows:
                                    sums[row_tap] += value * grads[y - row_tap][part]
                    for r in range(side):
                        total[r * side + col_tap] = sums[r]

        each_frame(frames, one)
        out[...] = jnp.sum(total[...], axis=1)

    return call(
        body,
        (width // LANES,),
        [tile4(a) for a in (block, *pieces)] + [tile5(inner), tile5(outer)],
        [((out_rows, width), F32, (out_rows, LANES), lambda c: (0, c))],
        [
            pltpu.VMEM((rows + 2 * half, cols + 2 * EDGE, LANES), F32),
            pltpu.VMEM((rows, cols, LANES), F32),
            pltpu.VMEM((out_rows, 8, LANES), F32),
        ],
        flops=2 * side * side * block.size,
    )


def whole(a):
    return (a, a.shape, lambda i: (0,) * len(a.shape))


def made(shape):
    return (shape, BF16, shape, lambda i: (0,) * len(shape))


def group_grads(grads, groups):
    frames, rows, _, width = grads.shape
    size = rows // groups

    def body(g, out):
        for y in range(rows):
            for f in range(frames):
                x = g[f, y]
                out[y // size, 0, f, y % size] = x[8:24, :]
                out[y // size, 1, f, y % size] = jnp.concatenate([x[:8, :], x[24:, :]], axis=0)

    shape = (groups, 2, frames, size, 16, width)
    return call(body, (1,), [whole(grads)], [made(shape)])


def edge_rows(inner, outer, half):
    groups, frames, size, _, width = inner.shape
    rows = groups * size
    shape = (frames, half, 32, width)

    def body(i, o, top, bottom):
        for k in range(half):
            for out, y in ((top, k), (bottom, rows - half + k)):
                for f in range(frames):
                    at = (y // size, f, y % size)
                    out[f, k, 0:16, :] = i[at]
                    out[f, k, 16:32, :] = o[at]

    return call(body, (1,), [whole(inner), whole(outer)], [made(shape), made(shape)])


def edge_columns(outer, above, below, half):
    groups, frames, size, _, width = outer.shape
    rows = groups * size
    shape = (frames, rows + 2 * half, half, width)

    def body(o, n, s, left, right):
        for y in range(rows + 2 * half):
            for f in range(frames):
                if y < half:
                    line = n[f, y, 16:32, :]
                elif y < half + rows:
                    line = o[(y - half) // size, f, (y - half) % size]
                else:
                    line = s[f, y - half - rows, 16:32, :]
                left[f, y] = line[:half]
                right[f, y] = line[16 - half :]

    return call(body, (1,), [whole(outer), whole(above), whole(below)], [made(shape), made(shape)])


def dot(a, b, over):
    return lax.dot_general(a, b, ((over[:1], over[1:]), ((), ())), preferred_element_type=F32)


def attend_body(x, g, w_qkv, w_out, token_grad, stacked, attended):
    cells, width = x.shape[3:]
    rows = x.shape[0] * x.shape[1] * cells
    depth = width // HEADS
    scale = depth ** (-0.5)
    mixed = x[...].reshape(rows, width)
    grads = g[...].reshape(rows, width)
    projected = dot(mixed, w_qkv[...], (1, 0)).astype(BF16)
    grad_att = dot(grads, w_out[...], (1, 1)).astype(BF16)
    at_row = lax.broadcasted_iota(jnp.int32, (rows, rows), 0)
    at_col = lax.broadcasted_iota(jnp.int32, (rows, rows), 1)
    same = lax.rem(at_row, cells) == lax.rem(at_col, cells)
    attended_parts, query_parts, key_parts, value_parts = [], [], [], []
    for head in range(HEADS):
        at = head * depth
        query = projected[:, at : at + depth]
        key = projected[:, width + at : width + at + depth]
        value = projected[:, 2 * width + at : 2 * width + at + depth]
        grad_a = grad_att[:, at : at + depth]
        scores = dot(key, query, (1, 1)) * scale
        raised = jnp.exp(jnp.where(same, scores, -jnp.inf))
        probs = raised * (1.0 / jnp.sum(raised, axis=0, keepdims=True))
        low = probs.astype(BF16)
        attended_parts.append(dot(low, value, (0, 0)).astype(BF16))
        grad_probs = dot(value, grad_a, (1, 1))
        inner = jnp.sum(probs * grad_probs, axis=0, keepdims=True)
        grad_scores = (probs * (grad_probs - inner) * scale).astype(BF16)
        query_parts.append(dot(grad_scores, key, (0, 0)).astype(BF16))
        key_parts.append(dot(grad_scores, query, (1, 0)).astype(BF16))
        value_parts.append(dot(low, grad_a, (1, 0)).astype(BF16))
    attended[...] = jnp.concatenate(attended_parts, axis=1).reshape(attended.shape)
    grad_qkv = jnp.concatenate(query_parts + key_parts + value_parts, axis=1)
    stacked[...] = grad_qkv.reshape(stacked.shape)
    back = dot(grad_qkv, w_qkv[...], (1, 1)).astype(BF16)
    token_grad[...] = back.reshape(token_grad.shape)


def attend(mixed, grads, chunk, w_qkv, w_out):
    groups, frames, size, cols, width = mixed.shape
    tokens = groups * frames * size * cols

    def spot(i):
        return (0, 0, i, 0, 0)

    def rows_of(columns):
        return (groups, frames, 1, cols, columns)

    def all_of(columns):
        return (groups, frames, size, cols, columns)

    return call(
        attend_body,
        (size,),
        [
            (mixed, rows_of(width), spot),
            (
                grads,
                (groups, None, frames, 1, cols, width),
                lambda i: (0, chunk, 0, i, 0, 0),
            ),
            (w_qkv, w_qkv.shape, lambda i: (0, 0)),
            (w_out, w_out.shape, lambda i: (0, 0)),
        ],
        [(all_of(c), BF16, rows_of(c), spot) for c in (width, 3 * width, width)],
        flops=2 * tokens * width * width * 8,
    )


def weight_terms(core, mixed, stacked, attended, grads):
    groups, frames, size, cols, width = mixed[0].shape
    tokens = groups * frames * size * cols
    quarter = width // 4

    def body(core, *refs):
        x, (s0, s1), a, (g0, g1), (other, own) = (
            refs[0:4], refs[4:6], refs[6:10], refs[10:12], refs[12:14]
        )
        step = pl.program_id(0)

        def emit(out):
            x0 = jnp.concatenate([x[0][...], x[1][...]], axis=1)
            x1 = jnp.concatenate([x[2][...], x[3][...]], axis=1)
            a0 = jnp.concatenate([a[0][...], a[1][...]], axis=1)
            a1 = jnp.concatenate([a[2][...], a[3][...]], axis=1)
            qkv = dot(x0, s0[...], (0, 0)) + dot(x1, s1[...], (0, 0))
            last = dot(a0, g0[...].reshape(tokens, width), (0, 0)) + dot(
                a1, g1[...].reshape(tokens, width), (0, 0)
            )
            for upper in range(2):
                rows = slice(upper * quarter, (upper + 1) * quarter)
                out[upper, :, 0 : 3 * width] = qkv[rows].astype(out.dtype)
                out[upper, :, 3 * width :] = last[rows].astype(out.dtype)

        @pl.when(step == 0)
        def _():
            emit(other)

        @pl.when(step == 1)
        def _():
            emit(own)

    def some(upper):
        return lambda i, c: (0, 2 * upper + jnp.where(i == 0, 1 - c[0], c[0]))

    def every(i, c):
        return (0, 0)

    flat = lambda a: a.reshape(tokens, a.shape[-1])
    ins = [(flat(a), (tokens, quarter), some(upper)) for a in mixed for upper in range(2)]
    ins += [(flat(a), (tokens, 3 * width), every) for a in stacked]
    ins += [(flat(a), (tokens, quarter), some(upper)) for a in attended for upper in range(2)]
    part = (groups, None, frames, size, cols, width)
    ins += [
        (grads, part, lambda i, c: (0, 0, 0, 0, 0, 0)),
        (grads, part, lambda i, c: (0, 1, 0, 0, 0, 0)),
    ]
    shape = (2, quarter, 4 * width)
    return call(
        body,
        (2,),
        ins,
        [(shape, dtype, shape, lambda i, c: (0, 0, 0)) for dtype in (BF16, F32)],
        flops=4 * tokens * width * width * 4,
        arrays=(core.reshape(1).astype(jnp.int32),),
        prefetch=1,
    )


def chip_sum(own, pair, lats, lons):
    upper, rows, width = own.shape
    each = rows // (lats * lons)
    part = width // 4

    def body(a, b, out):
        for half in range(upper):
            total = a[half] + b[half].astype(F32)
            for lon in range(lons):
                starts = [(lat * lons + lon) * each for lat in range(lats)]
                pieces = [total[at : at + each] for at in starts]
                out[lon, half] = jnp.concatenate(pieces, axis=0).astype(BF16)

    shape = (lons, upper, lats * each, width)
    spot = lambda i: (0, 0, i)
    return call(
        body,
        (4,),
        [(a, (upper, rows, part), spot) for a in (own, pair)],
        [(shape, BF16, shape[:3] + (part,), lambda i: (0, 0, 0, i))],
    )


def exchange(a, axis):
    return lax.all_to_all(a, axis, split_axis=0, concat_axis=0, tiled=True)


def on_device(frames_in, grad_out, kernel, w_qkv, w_out):
    local_frames, tile_lat, tile_lon, width = frames_in.shape
    half = math.isqrt(kernel.shape[0]) // 2
    frame_index = lax.axis_index("frame")
    core = lax.rem(frame_index, 2)
    clip_groups = lax.axis_size("frame")
    lats, lons = lax.axis_size("lat"), lax.axis_size("lon")

    top, bottom = frames_in[:, :half], frames_in[:, tile_lat - half :]
    above, below = rows_around(top, bottom)
    grouped = group_grads(grad_out, clip_groups)
    grads = exchange(grouped, "frame")
    left, right = ends((above, frames_in, below), half)
    sides = columns_around(left, right)
    mixed_inner = conv_forward(frames_in, above, below, (), kernel, clip_groups)
    inner = exchange(mixed_inner, "frame")
    mixed_outer = conv_forward(frames_in, above, below, sides, kernel, clip_groups)
    outer = exchange(mixed_outer, "frame")
    back_inner, stacked_inner, attended_inner = attend(inner, grads, 0, w_qkv, w_out)
    grad_inner = exchange(back_inner, "frame")
    back_outer, stacked_outer, attended_outer = attend(outer, grads, 1, w_qkv, w_out)
    grad_outer = exchange(back_outer, "frame")

    terms_other, terms_own = weight_terms(
        core,
        (inner, outer),
        (stacked_inner, stacked_outer),
        (attended_inner, attended_outer),
        grads,
    )
    swap = [(i, i ^ 1) for i in range(clip_groups)]
    terms_pair = lax.ppermute(terms_other, "frame", swap)
    cells = chip_sum(terms_own, terms_pair, lats, lons)
    cells = exchange(cells, "lon")
    cells = jnp.sum(cells.astype(F32), axis=0).reshape(2, lats, -1, width).swapaxes(0, 1)
    parity = lax.rem(jnp.arange(clip_groups), 2)[:, None, None, None] == core
    cells = jnp.where(parity, jnp.repeat(cells.swapaxes(0, 1), clip_groups // 2, axis=0), 0.0)
    cells = cells.reshape((clip_groups * lats,) + cells.shape[2:]).astype(BF16)

    top, bottom = edge_rows(grad_inner, grad_outer, half)
    grad_above, grad_below = rows_around(top, bottom)
    kernel_part = tap_products(
        frames_in, (above, below, *sides), grad_inner, grad_outer, 56
    )
    rows = kernel_part.shape[0]

    def to_all(a, count):
        return jnp.broadcast_to(a[None], (count,) + a.shape)

    joined = [to_all(kernel_part.astype(BF16), clip_groups * lats), cells]
    joined = jnp.concatenate(joined, axis=1)
    parts = exchange(joined, ("frame", "lat"))
    left, right = edge_columns(grad_outer, grad_above, grad_below, half)
    grad_sides = columns_around(left, right)
    input_inner = conv_adjoint(
        grad_inner, grad_outer, grad_above, grad_below, (), kernel, grad_out, None
    )
    part_sum = jnp.sum(parts.reshape(joined.shape).astype(F32), axis=0)
    proj_sum = part_sum[rows:].reshape(-1, 4 * width)
    lon_parts = exchange(to_all(part_sum[:rows].astype(BF16), lons), "lon")
    grad_input = conv_adjoint(
        grad_inner, grad_outer, grad_above, grad_below, grad_sides, kernel, grad_out, input_inner
    )
    kernel_sum = jnp.sum(lon_parts.reshape(lons, rows, width).astype(F32), axis=0)
    kernel_sum = kernel_sum[: kernel.shape[0]]

    cells = local_frames * clip_groups * tile_lat * tile_lon * lats * lons
    scale = cells ** (-0.5)
    return (grad_input, proj_sum * scale, kernel_sum * scale)


def solution(mesh):
    in_specs = (P("frame", "lat", "lon", None), P("frame", "lat", "lon", None), P(), P(), P())
    out_specs = (P("frame", "lat", "lon", None), P(("frame", "lat", "lon"), None), P())

    return jax.shard_map(
        on_device, mesh=mesh, in_specs=in_specs, out_specs=out_specs, check_vma=False
    )
```

```python
import math

import jax
import jax.numpy as jnp
from jax import lax
from jax.experimental import pallas as pl
from jax.experimental.pallas import tpu as pltpu
from jax.sharding import PartitionSpec as P


HEADS = 4
LANES = 128
EDGE = 8
F32 = jnp.float32
BF16 = jnp.bfloat16


def shift(piece, axis, step):
    count = lax.axis_size(axis)
    pairs = [(i, i + step) for i in range(count) if 0 <= i + step < count]
    return lax.ppermute(piece, axis, pairs)


def rows_around(top, bottom):
    above = shift(bottom, "lat", 1)
    below = shift(top, "lat", -1)
    return above, below


def columns_around(left, right):
    before = shift(right, "lon", 1)
    after = shift(left, "lon", -1)
    return before, after


def ends(parts, half):
    cols = parts[0].shape[2]
    left = jnp.concatenate([a[:, :, :half] for a in parts], axis=1)
    right = jnp.concatenate([a[:, :, cols - half :] for a in parts], axis=1)
    return left, right


def call(body, grid, ins, outs, scratch=(), flops=0, arrays=None, prefetch=0):
    moved = sum(a.size * a.dtype.itemsize for a, _, _ in ins)
    moved += sum(math.prod(o[0]) * jnp.dtype(o[1]).itemsize for o in outs)
    results = pl.pallas_call(
        body,
        grid_spec=pltpu.PrefetchScalarGridSpec(
            num_scalar_prefetch=prefetch,
            grid=grid,
            in_specs=[pl.BlockSpec(block, index) for _, block, index in ins],
            out_specs=[pl.BlockSpec(block, index) for _, _, block, index in outs],
            scratch_shapes=scratch,
        ),
        out_shape=[jax.ShapeDtypeStruct(o[0], o[1]) for o in outs],
        cost_estimate=pl.CostEstimate(flops=flops, bytes_accessed=moved, transcendentals=0),
    )(*(arrays or ()), *[a for a, _, _ in ins])
    return results[0] if len(outs) == 1 else results


def in_vmem(body, ins, shapes):
    whole = pl.BlockSpec(memory_space=pltpu.VMEM)
    return pl.pallas_call(
        body,
        in_specs=[whole] * len(ins),
        out_specs=[whole] * len(shapes),
        out_shape=[jax.ShapeDtypeStruct(shape, BF16) for shape in shapes],
        compiler_params=pltpu.CompilerParams(vmem_limit_bytes=4 << 20),
        cost_estimate=pl.CostEstimate(
            flops=0, bytes_accessed=4 * sum(a.size for a in ins), transcendentals=0
        ),
    )(*ins)


INNER, OUTER = (8, 16), (0, 24)


def put(dst, y, col, value):
    for piece, at in enumerate(col):
        dst[y, at : at + 8, :] = value[8 * piece : 8 * piece + 8, :]


def fill_plain(pad, f, c, n, s, half):
    rows, cols = c.shape[1], c.shape[2]
    pad[half : half + rows, EDGE : EDGE + cols, :] = c[f].astype(F32)
    pad[0:half, EDGE : EDGE + cols, :] = n[f].astype(F32)
    pad[half + rows : rows + 2 * half, EDGE : EDGE + cols, :] = s[f].astype(F32)


def fill_sides(pad, f, w, e, half, cols):
    pad[:, EDGE - half : EDGE, :] = w[f].astype(F32)
    pad[:, EDGE + cols : EDGE + cols + half, :] = e[f].astype(F32)


def chunked_row(pad, y, inner, outer):
    put(pad, y, [EDGE + at for at in INNER], inner.astype(F32))
    put(pad, y, [EDGE + at for at in OUTER], outer.astype(F32))


def fill_chunked(pad, f, inner, outer, n, s, half):
    size = inner.shape[2]
    rows = inner.shape[0] * size
    for y in range(rows):
        at = (y // size, f, y % size)
        chunked_row(pad, half + y, inner[at], outer[at])
    for y in range(half):
        chunked_row(pad, y, n[f, y, 0:16, :], n[f, y, 16:32, :])
        chunked_row(pad, half + rows + y, s[f, y, 0:16, :], s[f, y, 16:32, :])


def each_frame(frames, step):
    lax.fori_loop(0, frames, lambda f, done: (step(f), done)[1], 0)


def conv_sums(pad, taps, rows, half, columns, flipped):
    side = 2 * half + 1
    sums = [[jnp.zeros((8, LANES), F32) for _ in columns] for _ in range(rows)]
    for col_tap in range(side):
        weights = []
        for row_tap in range(side):
            at = row_tap * side + col_tap
            if flipped:
                at = side * side - 1 - at
            weights.append(jnp.broadcast_to(taps[at : at + 1, :], (8, LANES)))
        for y in range(rows + side - 1):
            for part, col in enumerate(columns):
                first = EDGE - half + col + col_tap
                value = pad[y, first : first + 8, :]
                for row_tap in range(side):
                    if 0 <= y - row_tap < rows:
                        sums[y - row_tap][part] += weights[row_tap] * value
    return [jnp.concatenate(pair, axis=0) for pair in sums]


def wide_tap(kernel):
    return (kernel, (kernel.shape[0], LANES), lambda c: (0, c))


def tile4(a):
    return (a, a.shape[:3] + (LANES,), lambda c: (0, 0, 0, c))


def tile5(a):
    return (a, a.shape[:4] + (LANES,), lambda c: (0, 0, 0, 0, c))


def conv_scratch(rows, cols, half, taps):
    return [
        pltpu.VMEM((rows + 2 * half, cols + 2 * EDGE, LANES), F32),
        pltpu.VMEM((-(-taps // 8) * 8, LANES), F32),
    ]


def conv_forward(block, above, below, sides, kernel, groups):
    frames, rows, cols, width = block.shape
    count = kernel.shape[0]
    half = above.shape[1]
    size = rows // groups
    columns = OUTER if sides else INNER

    def body(c, n, s, *rest):
        if sides:
            w, e, k, out, pad, taps = rest
        else:
            k, out, pad, taps = rest
        taps[0:count, :] = k[...].astype(F32)

        def one(f):
            fill_plain(pad, f, c, n, s, half)
            if sides:
                fill_sides(pad, f, w, e, half, cols)
            for y, total in enumerate(conv_sums(pad, taps, rows, half, columns, False)):
                out[y // size, f, y % size] = total.astype(BF16)

        each_frame(frames, one)

    shape = (groups, frames, size, 16, width)
    return call(
        body,
        (width // LANES,),
        [tile4(a) for a in (block, above, below, *sides)] + [wide_tap(kernel)],
        [(shape, BF16) + tile5(jax.ShapeDtypeStruct(shape, BF16))[1:]],
        conv_scratch(rows, cols, half, count),
        flops=count * block.size,
    )


def conv_adjoint(inner, outer, above, below, sides, kernel, base, before):
    frames, rows, cols, width = base.shape
    count = kernel.shape[0]
    half = above.shape[1]
    columns = OUTER if sides else INNER

    def body(i, o, n, s, g, *rest):
        if sides:
            w, e, b, k, out, pad, taps = rest
        else:
            k, out, pad, taps = rest
        taps[0:count, :] = k[...].astype(F32)

        def one(f):
            fill_chunked(pad, f, i, o, n, s, half)
            if sides:
                fill_sides(pad, f, w, e, half, cols)
            for y, total in enumerate(conv_sums(pad, taps, rows, half, columns, True)):
                grads = g[f, y].astype(F32)
                grads = [grads[at : at + 8, :] for at in columns]
                total = total + jnp.concatenate(grads, axis=0)
                if sides:
                    pieces = [total[:8], b[f, y].astype(F32), total[8:]]
                    total = jnp.concatenate(pieces, axis=0)
                out[f, y] = total.astype(BF16)

        each_frame(frames, one)

    shape = base.shape if sides else (frames, rows, 16, width)
    extra = [tile4(a) for a in (*sides, before)] if sides else []
    return call(
        body,
        (width // LANES,),
        [tile5(inner), tile5(outer), tile4(above), tile4(below), tile4(base)]
        + extra
        + [wide_tap(kernel)],
        [(shape, BF16) + tile4(jax.ShapeDtypeStruct(shape, BF16))[1:]],
        conv_scratch(rows, cols, half, count),
        flops=count * base.size,
    )


def tap_products(block, pieces, inner, outer, out_rows, copies):
    frames, rows, cols, width = block.shape
    half = pieces[0].shape[1]
    side = 2 * half + 1
    size = inner.shape[2]

    def body(c, n, s, w, e, i, o, out, pad, wide, total):
        total[...] = jnp.zeros_like(total)

        def one(f):
            fill_plain(pad, f, c, n, s, half)
            fill_sides(pad, f, w, e, half, cols)
            for y in range(rows):
                at = (y // size, f, y % size)
                put(wide, y, INNER, i[at].astype(F32))
                put(wide, y, OUTER, o[at].astype(F32))
            for col in range(0, cols, 16):
                grads = [
                    [wide[y, col + 8 * part : col + 8 * part + 8, :] for part in range(2)]
                    for y in range(rows)
                ]
                for col_tap in range(side):
                    sums = [total[r * side + col_tap] for r in range(side)]
                    for y in range(rows + side - 1):
                        for part in range(2):
                            first = EDGE - half + col + 8 * part + col_tap
                            value = pad[y, first : first + 8, :]
                            for row_tap in range(side):
                                if 0 <= y - row_tap < rows:
                                    sums[row_tap] += value * grads[y - row_tap][part]
                    for r in range(side):
                        total[r * side + col_tap] = sums[r]

        each_frame(frames, one)
        terms = jnp.sum(total[...], axis=1).astype(BF16)
        for copy in range(copies):
            out[copy] = terms

    return call(
        body,
        (width // LANES,),
        [tile4(a) for a in (block, *pieces)] + [tile5(inner), tile5(outer)],
        [
            (
                (copies, out_rows, width),
                BF16,
                (copies, out_rows, LANES),
                lambda c: (0, 0, c),
            )
        ],
        [
            pltpu.VMEM((rows + 2 * half, cols + 2 * EDGE, LANES), F32),
            pltpu.VMEM((rows, cols, LANES), F32),
            pltpu.VMEM((out_rows, 8, LANES), F32),
        ],
        flops=2 * side * side * block.size,
    )


def group_grads(grads, groups):
    frames, rows, _, width = grads.shape
    size = rows // groups

    def body(g, out):
        for y in range(rows):
            for f in range(frames):
                x = g[f, y]
                out[y // size, 0, f, y % size] = x[8:24, :]
                out[y // size, 1, f, y % size] = jnp.concatenate([x[:8, :], x[24:, :]], axis=0)

    shape = (groups, 2, frames, size, 16, width)
    return in_vmem(body, [grads], [shape])[0]


def edge_rows(inner, outer, half):
    groups, frames, size, _, width = inner.shape
    rows = groups * size
    shape = (frames, half, 32, width)

    def body(i, o, top, bottom):
        for k in range(half):
            for out, y in ((top, k), (bottom, rows - half + k)):
                for f in range(frames):
                    at = (y // size, f, y % size)
                    out[f, k, 0:16, :] = i[at]
                    out[f, k, 16:32, :] = o[at]

    return in_vmem(body, [inner, outer], [shape, shape])


def edge_columns(outer, above, below, half):
    groups, frames, size, _, width = outer.shape
    rows = groups * size
    shape = (frames, rows + 2 * half, half, width)

    def body(o, n, s, left, right):
        for y in range(rows + 2 * half):
            for f in range(frames):
                if y < half:
                    line = n[f, y, 16:32, :]
                elif y < half + rows:
                    line = o[(y - half) // size, f, (y - half) % size]
                else:
                    line = s[f, y - half - rows, 16:32, :]
                left[f, y] = line[:half]
                right[f, y] = line[16 - half :]

    return in_vmem(body, [outer, above, below], [shape, shape])


def join_terms(parts, cells):
    count, rows, width = parts.shape
    receivers, first, _ = cells.shape

    def body(p, c, out):
        total = p[0].astype(F32)
        for i in range(1, count):
            total = total + p[i].astype(F32)
        total = total.astype(BF16)
        for i in range(receivers):
            out[i, 0:first, :] = c[i]
            out[i, first : first + rows, :] = total

    return in_vmem(body, [parts, cells], [(receivers, first + rows, width)])[0]


def dot(a, b, over):
    return lax.dot_general(a, b, ((over[:1], over[1:]), ((), ())), preferred_element_type=F32)


def attend_body(x, g, w_qkv, w_out, token_grad, stacked, attended):
    cells, width = x.shape[3:]
    rows = x.shape[0] * x.shape[1] * cells
    depth = width // HEADS
    scale = depth ** (-0.5)
    mixed = x[...].reshape(rows, width)
    grads = g[...].reshape(rows, width)
    projected = dot(mixed, w_qkv[...], (1, 0)).astype(BF16)
    grad_att = dot(grads, w_out[...], (1, 1)).astype(BF16)
    at_row = lax.broadcasted_iota(jnp.int32, (rows, rows), 0)
    at_col = lax.broadcasted_iota(jnp.int32, (rows, rows), 1)
    same = lax.rem(at_row, cells) == lax.rem(at_col, cells)
    attended_parts, query_parts, key_parts, value_parts = [], [], [], []
    for head in range(HEADS):
        at = head * depth
        query = projected[:, at : at + depth]
        key = projected[:, width + at : width + at + depth]
        value = projected[:, 2 * width + at : 2 * width + at + depth]
        grad_a = grad_att[:, at : at + depth]
        scores = dot(key, query, (1, 1)) * scale
        raised = jnp.exp(jnp.where(same, scores, -jnp.inf))
        probs = raised * (1.0 / jnp.sum(raised, axis=0, keepdims=True))
        low = probs.astype(BF16)
        attended_parts.append(dot(low, value, (0, 0)).astype(BF16))
        grad_probs = dot(value, grad_a, (1, 1))
        inner = jnp.sum(probs * grad_probs, axis=0, keepdims=True)
        grad_scores = (probs * (grad_probs - inner) * scale).astype(BF16)
        query_parts.append(dot(grad_scores, key, (0, 0)).astype(BF16))
        key_parts.append(dot(grad_scores, query, (1, 0)).astype(BF16))
        value_parts.append(dot(low, grad_a, (1, 0)).astype(BF16))
    attended[...] = jnp.concatenate(attended_parts, axis=1).reshape(attended.shape)
    grad_qkv = jnp.concatenate(query_parts + key_parts + value_parts, axis=1)
    stacked[...] = grad_qkv.reshape(stacked.shape)
    back = dot(grad_qkv, w_qkv[...], (1, 1)).astype(BF16)
    token_grad[...] = back.reshape(token_grad.shape)


def attend(mixed, grads, chunk, w_qkv, w_out):
    groups, frames, size, cols, width = mixed.shape
    tokens = groups * frames * size * cols

    def spot(i):
        return (0, 0, i, 0, 0)

    def rows_of(columns):
        return (groups, frames, 1, cols, columns)

    def all_of(columns):
        return (groups, frames, size, cols, columns)

    return call(
        attend_body,
        (size,),
        [
            (mixed, rows_of(width), spot),
            (
                grads,
                (groups, None, frames, 1, cols, width),
                lambda i: (0, chunk, 0, i, 0, 0),
            ),
            (w_qkv, w_qkv.shape, lambda i: (0, 0)),
            (w_out, w_out.shape, lambda i: (0, 0)),
        ],
        [(all_of(c), BF16, rows_of(c), spot) for c in (width, 3 * width, width)],
        flops=2 * tokens * width * width * 8,
    )


def weight_terms(core, mixed, stacked, attended, grads):
    groups, frames, size, cols, width = mixed[0].shape
    tokens = groups * frames * size * cols
    quarter = width // 4

    def body(core, *refs):
        x, (s0, s1), a, (g0, g1), (other, own) = (
            refs[0:4], refs[4:6], refs[6:10], refs[10:12], refs[12:14]
        )
        step = pl.program_id(0)

        def emit(out):
            x0 = jnp.concatenate([x[0][...], x[1][...]], axis=1)
            x1 = jnp.concatenate([x[2][...], x[3][...]], axis=1)
            a0 = jnp.concatenate([a[0][...], a[1][...]], axis=1)
            a1 = jnp.concatenate([a[2][...], a[3][...]], axis=1)
            qkv = dot(x0, s0[...], (0, 0)) + dot(x1, s1[...], (0, 0))
            last = dot(a0, g0[...].reshape(tokens, width), (0, 0)) + dot(
                a1, g1[...].reshape(tokens, width), (0, 0)
            )
            for upper in range(2):
                rows = slice(upper * quarter, (upper + 1) * quarter)
                out[upper, :, 0 : 3 * width] = qkv[rows].astype(out.dtype)
                out[upper, :, 3 * width :] = last[rows].astype(out.dtype)

        @pl.when(step == 0)
        def _():
            emit(other)

        @pl.when(step == 1)
        def _():
            emit(own)

    def some(upper):
        return lambda i, c: (0, 2 * upper + jnp.where(i == 0, 1 - c[0], c[0]))

    def every(i, c):
        return (0, 0)

    flat = lambda a: a.reshape(tokens, a.shape[-1])
    ins = [(flat(a), (tokens, quarter), some(upper)) for a in mixed for upper in range(2)]
    ins += [(flat(a), (tokens, 3 * width), every) for a in stacked]
    ins += [(flat(a), (tokens, quarter), some(upper)) for a in attended for upper in range(2)]
    part = (groups, None, frames, size, cols, width)
    ins += [
        (grads, part, lambda i, c: (0, 0, 0, 0, 0, 0)),
        (grads, part, lambda i, c: (0, 1, 0, 0, 0, 0)),
    ]
    shape = (2, quarter, 4 * width)
    return call(
        body,
        (2,),
        ins,
        [(shape, dtype, shape, lambda i, c: (0, 0, 0)) for dtype in (BF16, F32)],
        flops=4 * tokens * width * width * 4,
        arrays=(core.reshape(1).astype(jnp.int32),),
        prefetch=1,
    )


def chip_sum(own, pair, lats, lons):
    upper, rows, width = own.shape
    each = rows // (lats * lons)
    part = width // 2

    def body(a, b, out):
        for half in range(upper):
            total = a[half] + b[half].astype(F32)
            for lon in range(lons):
                starts = [(lat * lons + lon) * each for lat in range(lats)]
                pieces = [total[at : at + each] for at in starts]
                out[lon, half] = jnp.concatenate(pieces, axis=0).astype(BF16)

    shape = (lons, upper, lats * each, width)
    spot = lambda i: (0, 0, i)
    return call(
        body,
        (2,),
        [(a, (upper, rows, part), spot) for a in (own, pair)],
        [(shape, BF16, shape[:3] + (part,), lambda i: (0, 0, 0, i))],
    )


def exchange(a, axis):
    return lax.all_to_all(a, axis, split_axis=0, concat_axis=0, tiled=True)


def on_device(frames_in, grad_out, kernel, w_qkv, w_out):
    local_frames, tile_lat, tile_lon, width = frames_in.shape
    half = math.isqrt(kernel.shape[0]) // 2
    frame_index = lax.axis_index("frame")
    core = lax.rem(frame_index, 2)
    clip_groups = lax.axis_size("frame")
    lats, lons = lax.axis_size("lat"), lax.axis_size("lon")

    top, bottom = frames_in[:, :half], frames_in[:, tile_lat - half :]
    above, below = rows_around(top, bottom)
    grouped = group_grads(grad_out, clip_groups)
    grads = exchange(grouped, "frame")
    left, right = ends((above, frames_in, below), half)
    sides = columns_around(left, right)
    mixed_inner = conv_forward(frames_in, above, below, (), kernel, clip_groups)
    inner = exchange(mixed_inner, "frame")
    mixed_outer = conv_forward(frames_in, above, below, sides, kernel, clip_groups)
    outer = exchange(mixed_outer, "frame")
    back_inner, stacked_inner, attended_inner = attend(inner, grads, 0, w_qkv, w_out)
    grad_inner = exchange(back_inner, "frame")
    back_outer, stacked_outer, attended_outer = attend(outer, grads, 1, w_qkv, w_out)
    grad_outer = exchange(back_outer, "frame")

    terms_other, terms_own = weight_terms(
        core,
        (inner, outer),
        (stacked_inner, stacked_outer),
        (attended_inner, attended_outer),
        grads,
    )
    swap = [(i, i ^ 1) for i in range(clip_groups)]
    terms_pair = lax.ppermute(terms_other, "frame", swap)
    cells = chip_sum(terms_own, terms_pair, lats, lons)
    cells = exchange(cells, "lon")
    cells = jnp.sum(cells.astype(F32), axis=0).reshape(2, lats, -1, width).swapaxes(0, 1)
    parity = lax.rem(jnp.arange(clip_groups), 2)[:, None, None, None] == core
    cells = jnp.where(parity, jnp.repeat(cells.swapaxes(0, 1), clip_groups // 2, axis=0), 0.0)
    cells = cells.reshape((clip_groups * lats,) + cells.shape[2:]).astype(BF16)

    top, bottom = edge_rows(grad_inner, grad_outer, half)
    grad_above, grad_below = rows_around(top, bottom)
    kernel_parts = tap_products(frames_in, (above, below, *sides), grad_inner, grad_outer, 56, lons)

    lon_parts = exchange(kernel_parts, "lon")
    left, right = edge_columns(grad_outer, grad_above, grad_below, half)
    grad_sides = columns_around(left, right)
    joined = join_terms(lon_parts.reshape(kernel_parts.shape), cells)
    parts = exchange(joined, ("frame", "lat"))
    input_inner = conv_adjoint(
        grad_inner, grad_outer, grad_above, grad_below, (), kernel, grad_out, None
    )
    grad_input = conv_adjoint(
        grad_inner, grad_outer, grad_above, grad_below, grad_sides, kernel, grad_out, input_inner
    )
    part_sum = jnp.sum(parts.reshape(joined.shape).astype(F32), axis=0)
    rows = cells.shape[1]
    kernel_sum = part_sum[rows : rows + kernel.shape[0]]
    proj_sum = part_sum[:rows].reshape(-1, 4 * width)

    cells = local_frames * clip_groups * tile_lat * tile_lon * lats * lons
    scale = cells ** (-0.5)
    return (grad_input, proj_sum * scale, kernel_sum * scale)


def solution(mesh):
    in_specs = (P("frame", "lat", "lon", None), P("frame", "lat", "lon", None), P(), P(), P())
    out_specs = (P("frame", "lat", "lon", None), P(("frame", "lat", "lon"), None), P())

    return jax.shard_map(
        on_device, mesh=mesh, in_specs=in_specs, out_specs=out_specs, check_vma=False
    )
```

```python
import math

import jax
import jax.numpy as jnp
from jax import lax
from jax.experimental import pallas as pl
from jax.experimental.pallas import tpu as pltpu
from jax.sharding import PartitionSpec as P


HEADS = 4
LANES = 128
EDGE = 8
F32 = jnp.float32
BF16 = jnp.bfloat16


def shift(piece, axis, step):
    count = lax.axis_size(axis)
    pairs = [(i, i + step) for i in range(count) if 0 <= i + step < count]
    return lax.ppermute(piece, axis, pairs)


def rows_around(top, bottom):
    above = shift(bottom, "lat", 1)
    below = shift(top, "lat", -1)
    return above, below


def columns_around(left, right):
    before = shift(right, "lon", 1)
    after = shift(left, "lon", -1)
    return before, after


def ends(parts, half):
    cols = parts[0].shape[2]
    left = jnp.concatenate([a[:, :, :half] for a in parts], axis=1)
    right = jnp.concatenate([a[:, :, cols - half :] for a in parts], axis=1)
    return left, right


def call(body, grid, ins, outs, scratch=(), flops=0, arrays=None, prefetch=0):
    moved = sum(a.size * a.dtype.itemsize for a, _, _ in ins)
    moved += sum(math.prod(o[0]) * jnp.dtype(o[1]).itemsize for o in outs)
    results = pl.pallas_call(
        body,
        grid_spec=pltpu.PrefetchScalarGridSpec(
            num_scalar_prefetch=prefetch,
            grid=grid,
            in_specs=[pl.BlockSpec(block, index) for _, block, index in ins],
            out_specs=[pl.BlockSpec(block, index) for _, _, block, index in outs],
            scratch_shapes=scratch,
        ),
        out_shape=[jax.ShapeDtypeStruct(o[0], o[1]) for o in outs],
        cost_estimate=pl.CostEstimate(flops=flops, bytes_accessed=moved, transcendentals=0),
    )(*(arrays or ()), *[a for a, _, _ in ins])
    return results[0] if len(outs) == 1 else results


def in_vmem(body, ins, shapes, scalars=()):
    whole = pl.BlockSpec(memory_space=pltpu.VMEM)
    return pl.pallas_call(
        body,
        in_specs=[pl.BlockSpec(memory_space=pltpu.SMEM) for _ in scalars] + [whole] * len(ins),
        out_specs=[whole] * len(shapes),
        out_shape=[jax.ShapeDtypeStruct(shape, BF16) for shape in shapes],
        compiler_params=pltpu.CompilerParams(vmem_limit_bytes=4 << 20),
        cost_estimate=pl.CostEstimate(
            flops=0, bytes_accessed=4 * sum(a.size for a in ins), transcendentals=0
        ),
    )(*scalars, *ins)


INNER, OUTER = (8, 16), (0, 24)


def put(dst, y, col, value):
    for piece, at in enumerate(col):
        dst[y, at : at + 8, :] = value[8 * piece : 8 * piece + 8, :]


def fill_plain(pad, f, c, n, s, half):
    rows, cols = c.shape[1], c.shape[2]
    pad[half : half + rows, EDGE : EDGE + cols, :] = c[f].astype(F32)
    pad[0:half, EDGE : EDGE + cols, :] = n[f].astype(F32)
    pad[half + rows : rows + 2 * half, EDGE : EDGE + cols, :] = s[f].astype(F32)


def fill_sides(pad, f, w, e, half, cols):
    pad[:, EDGE - half : EDGE, :] = w[f].astype(F32)
    pad[:, EDGE + cols : EDGE + cols + half, :] = e[f].astype(F32)


def chunked_row(pad, y, inner, outer):
    put(pad, y, [EDGE + at for at in INNER], inner.astype(F32))
    put(pad, y, [EDGE + at for at in OUTER], outer.astype(F32))


def fill_chunked(pad, f, inner, outer, n, s, half):
    size = inner.shape[2]
    rows = inner.shape[0] * size
    for y in range(rows):
        at = (y // size, f, y % size)
        chunked_row(pad, half + y, inner[at], outer[at])
    for y in range(half):
        chunked_row(pad, y, n[f, y, 0:16, :], n[f, y, 16:32, :])
        chunked_row(pad, half + rows + y, s[f, y, 0:16, :], s[f, y, 16:32, :])


def each_frame(frames, step):
    lax.fori_loop(0, frames, lambda f, done: (step(f), done)[1], 0)


def conv_sums(pad, taps, rows, half, columns, flipped):
    side = 2 * half + 1
    sums = [[jnp.zeros((8, LANES), F32) for _ in columns] for _ in range(rows)]
    for col_tap in range(side):
        weights = []
        for row_tap in range(side):
            at = row_tap * side + col_tap
            if flipped:
                at = side * side - 1 - at
            weights.append(jnp.broadcast_to(taps[at : at + 1, :], (8, LANES)))
        for y in range(rows + side - 1):
            for part, col in enumerate(columns):
                first = EDGE - half + col + col_tap
                value = pad[y, first : first + 8, :]
                for row_tap in range(side):
                    if 0 <= y - row_tap < rows:
                        sums[y - row_tap][part] += weights[row_tap] * value
    return [jnp.concatenate(pair, axis=0) for pair in sums]


def wide_tap(kernel):
    return (kernel, (kernel.shape[0], LANES), lambda c: (0, c))


def tile4(a):
    return (a, a.shape[:3] + (LANES,), lambda c: (0, 0, 0, c))


def tile5(a):
    return (a, a.shape[:4] + (LANES,), lambda c: (0, 0, 0, 0, c))


def conv_scratch(rows, cols, half, taps):
    return [
        pltpu.VMEM((rows + 2 * half, cols + 2 * EDGE, LANES), F32),
        pltpu.VMEM((-(-taps // 8) * 8, LANES), F32),
    ]


def conv_forward(block, above, below, sides, kernel, groups):
    frames, rows, cols, width = block.shape
    count = kernel.shape[0]
    half = above.shape[1]
    size = rows // groups
    columns = OUTER if sides else INNER

    def body(c, n, s, *rest):
        if sides:
            w, e, k, out, pad, taps = rest
        else:
            k, out, pad, taps = rest
        taps[0:count, :] = k[...].astype(F32)

        def one(f):
            fill_plain(pad, f, c, n, s, half)
            if sides:
                fill_sides(pad, f, w, e, half, cols)
            for y, total in enumerate(conv_sums(pad, taps, rows, half, columns, False)):
                out[y // size, f, y % size] = total.astype(BF16)

        each_frame(frames, one)

    shape = (groups, frames, size, 16, width)
    return call(
        body,
        (width // LANES,),
        [tile4(a) for a in (block, above, below, *sides)] + [wide_tap(kernel)],
        [(shape, BF16) + tile5(jax.ShapeDtypeStruct(shape, BF16))[1:]],
        conv_scratch(rows, cols, half, count),
        flops=count * block.size,
    )


def conv_adjoint(inner, outer, above, below, sides, kernel, base, before):
    frames, rows, cols, width = base.shape
    count = kernel.shape[0]
    half = above.shape[1]
    columns = OUTER if sides else INNER

    def body(i, o, n, s, g, *rest):
        if sides:
            w, e, b, k, out, pad, taps = rest
        else:
            k, out, pad, taps = rest
        taps[0:count, :] = k[...].astype(F32)

        def one(f):
            fill_chunked(pad, f, i, o, n, s, half)
            if sides:
                fill_sides(pad, f, w, e, half, cols)
            for y, total in enumerate(conv_sums(pad, taps, rows, half, columns, True)):
                grads = g[f, y].astype(F32)
                grads = [grads[at : at + 8, :] for at in columns]
                total = total + jnp.concatenate(grads, axis=0)
                if sides:
                    pieces = [total[:8], b[f, y].astype(F32), total[8:]]
                    total = jnp.concatenate(pieces, axis=0)
                out[f, y] = total.astype(BF16)

        each_frame(frames, one)

    shape = base.shape if sides else (frames, rows, 16, width)
    extra = [tile4(a) for a in (*sides, before)] if sides else []
    return call(
        body,
        (width // LANES,),
        [tile5(inner), tile5(outer), tile4(above), tile4(below), tile4(base)]
        + extra
        + [wide_tap(kernel)],
        [(shape, BF16) + tile4(jax.ShapeDtypeStruct(shape, BF16))[1:]],
        conv_scratch(rows, cols, half, count),
        flops=count * base.size,
    )


def tap_products(block, pieces, inner, outer, out_rows, copies):
    frames, rows, cols, width = block.shape
    half = pieces[0].shape[1]
    side = 2 * half + 1
    size = inner.shape[2]

    def body(c, n, s, w, e, i, o, out, pad, wide, total):
        total[...] = jnp.zeros_like(total)

        def one(f):
            fill_plain(pad, f, c, n, s, half)
            fill_sides(pad, f, w, e, half, cols)
            for y in range(rows):
                at = (y // size, f, y % size)
                put(wide, y, INNER, i[at].astype(F32))
                put(wide, y, OUTER, o[at].astype(F32))
            for col in range(0, cols, 16):
                grads = [
                    [wide[y, col + 8 * part : col + 8 * part + 8, :] for part in range(2)]
                    for y in range(rows)
                ]
                for col_tap in range(side):
                    sums = [total[r * side + col_tap] for r in range(side)]
                    for y in range(rows + side - 1):
                        for part in range(2):
                            first = EDGE - half + col + 8 * part + col_tap
                            value = pad[y, first : first + 8, :]
                            for row_tap in range(side):
                                if 0 <= y - row_tap < rows:
                                    sums[row_tap] += value * grads[y - row_tap][part]
                    for r in range(side):
                        total[r * side + col_tap] = sums[r]

        each_frame(frames, one)
        terms = jnp.sum(total[...], axis=1).astype(BF16)
        for copy in range(copies):
            out[copy] = terms

    return call(
        body,
        (width // LANES,),
        [tile4(a) for a in (block, *pieces)] + [tile5(inner), tile5(outer)],
        [
            (
                (copies, out_rows, width),
                BF16,
                (copies, out_rows, LANES),
                lambda c: (0, 0, c),
            )
        ],
        [
            pltpu.VMEM((rows + 2 * half, cols + 2 * EDGE, LANES), F32),
            pltpu.VMEM((rows, cols, LANES), F32),
            pltpu.VMEM((out_rows, 8, LANES), F32),
        ],
        flops=2 * side * side * block.size,
    )


def group_grads(grads, groups):
    frames, rows, _, width = grads.shape
    size = rows // groups

    def body(g, out):
        for y in range(rows):
            for f in range(frames):
                x = g[f, y]
                out[y // size, 0, f, y % size] = x[8:24, :]
                out[y // size, 1, f, y % size] = jnp.concatenate([x[:8, :], x[24:, :]], axis=0)

    shape = (groups, 2, frames, size, 16, width)
    return in_vmem(body, [grads], [shape])[0]


def edge_rows(inner, outer, half):
    groups, frames, size, _, width = inner.shape
    rows = groups * size
    shape = (frames, half, 32, width)

    def body(i, o, top, bottom):
        for k in range(half):
            for out, y in ((top, k), (bottom, rows - half + k)):
                for f in range(frames):
                    at = (y // size, f, y % size)
                    out[f, k, 0:16, :] = i[at]
                    out[f, k, 16:32, :] = o[at]

    return in_vmem(body, [inner, outer], [shape, shape])


def edge_columns(outer, above, below, half):
    groups, frames, size, _, width = outer.shape
    rows = groups * size
    shape = (frames, rows + 2 * half, half, width)

    def body(o, n, s, left, right):
        for y in range(rows + 2 * half):
            for f in range(frames):
                if y < half:
                    line = n[f, y, 16:32, :]
                elif y < half + rows:
                    line = o[(y - half) // size, f, (y - half) % size]
                else:
                    line = s[f, y - half - rows, 16:32, :]
                left[f, y] = line[:half]
                right[f, y] = line[16 - half :]

    return in_vmem(body, [outer, above, below], [shape, shape])


def join_terms(core, parts, cells, lats):
    count, rows, width = parts.shape
    senders, upper, lines, _ = cells.shape
    each = lines // lats
    first = 4 * each

    def body(own, p, c, out):
        total = p[0].astype(F32)
        for i in range(1, count):
            total = total + p[i].astype(F32)
        total = total.astype(BF16)
        for half in range(upper):
            terms = c[0, half].astype(F32)
            for i in range(1, senders):
                terms = terms + c[i, half].astype(F32)
            for lat in range(lats):
                lines = terms[lat * each : (lat + 1) * each]
                lines = [lines[:, q * width : (q + 1) * width] for q in range(4)]
                lines = jnp.concatenate(lines, axis=0)
                for parity in range(2):
                    at = (2 * half + parity) * lats + lat
                    kept = jnp.where(own[0] == parity, lines, 0.0)
                    out[at, 0:first, :] = kept.astype(BF16)
                    out[at, first : first + rows, :] = total

    shape = (2 * upper * lats, first + rows, width)
    scalars = [core.reshape(1).astype(jnp.int32)]
    return in_vmem(body, [parts, cells], [shape], scalars)[0]


def dot(a, b, over):
    return lax.dot_general(a, b, ((over[:1], over[1:]), ((), ())), preferred_element_type=F32)


def attend_body(x, g, w_qkv, w_out, token_grad, stacked, attended):
    groups, frames, size, cells, width = x.shape
    rows = groups * frames * cells
    depth = width // HEADS
    scale = depth ** (-0.5)

    def lines(ref):
        return jnp.concatenate([ref[:, :, y].reshape(rows, width) for y in range(size)], axis=0)

    def keep(ref, value):
        for y in range(size):
            part = value[y * rows : (y + 1) * rows]
            ref[:, :, y] = part.reshape(groups, frames, cells, value.shape[1])

    all_projected = dot(lines(x), w_qkv[...], (1, 0)).astype(BF16)
    all_grad_att = dot(lines(g), w_out[...], (1, 1)).astype(BF16)
    at_row = lax.broadcasted_iota(jnp.int32, (rows, rows), 0)
    at_col = lax.broadcasted_iota(jnp.int32, (rows, rows), 1)
    same = lax.rem(at_row, cells) == lax.rem(at_col, cells)
    attended_rows, grad_rows = [], []
    for y in range(size):
        projected = all_projected[y * rows : (y + 1) * rows]
        grad_att = all_grad_att[y * rows : (y + 1) * rows]
        attended_parts, query_parts, key_parts, value_parts = [], [], [], []
        for head in range(HEADS):
            at = head * depth
            query = projected[:, at : at + depth]
            key = projected[:, width + at : width + at + depth]
            value = projected[:, 2 * width + at : 2 * width + at + depth]
            grad_a = grad_att[:, at : at + depth]
            scores = dot(key, query, (1, 1)) * scale
            raised = jnp.exp(jnp.where(same, scores, -jnp.inf))
            probs = raised * (1.0 / jnp.sum(raised, axis=0, keepdims=True))
            low = probs.astype(BF16)
            attended_parts.append(dot(low, value, (0, 0)).astype(BF16))
            grad_probs = dot(value, grad_a, (1, 1))
            inner = jnp.sum(probs * grad_probs, axis=0, keepdims=True)
            grad_scores = (probs * (grad_probs - inner) * scale).astype(BF16)
            query_parts.append(dot(grad_scores, key, (0, 0)).astype(BF16))
            key_parts.append(dot(grad_scores, query, (1, 0)).astype(BF16))
            value_parts.append(dot(low, grad_a, (1, 0)).astype(BF16))
        attended_rows.append(jnp.concatenate(attended_parts, axis=1))
        grad_rows.append(jnp.concatenate(query_parts + key_parts + value_parts, axis=1))
    keep(attended, jnp.concatenate(attended_rows, axis=0))
    grad_qkv = jnp.concatenate(grad_rows, axis=0)
    keep(stacked, grad_qkv)
    keep(token_grad, dot(grad_qkv, w_qkv[...], (1, 1)).astype(BF16))


def attend(mixed, grads, chunk, w_qkv, w_out):
    groups, frames, size, cols, width = mixed.shape
    tokens = groups * frames * size * cols

    def spot(i):
        return (0, 0, 0, 0, 0)

    def rows_of(columns):
        return (groups, frames, size, cols, columns)

    def all_of(columns):
        return (groups, frames, size, cols, columns)

    return call(
        attend_body,
        (1,),
        [
            (mixed, rows_of(width), spot),
            (
                grads,
                (groups, None, frames, size, cols, width),
                lambda i: (0, chunk, 0, 0, 0, 0),
            ),
            (w_qkv, w_qkv.shape, lambda i: (0, 0)),
            (w_out, w_out.shape, lambda i: (0, 0)),
        ],
        [(all_of(c), BF16, rows_of(c), spot) for c in (width, 3 * width, width)],
        flops=2 * tokens * width * width * 8,
    )


def weight_terms(core, mixed, stacked, attended, grads):
    groups, frames, size, cols, width = mixed[0].shape
    tokens = groups * frames * size * cols
    quarter = width // 4

    def body(core, *refs):
        x, (s0, s1), a, (g0, g1), (other, own) = (
            refs[0:4], refs[4:6], refs[6:10], refs[10:12], refs[12:14]
        )
        step = pl.program_id(0)

        def emit(out):
            x0 = jnp.concatenate([x[0][...], x[1][...]], axis=1)
            x1 = jnp.concatenate([x[2][...], x[3][...]], axis=1)
            a0 = jnp.concatenate([a[0][...], a[1][...]], axis=1)
            a1 = jnp.concatenate([a[2][...], a[3][...]], axis=1)
            qkv = dot(x0, s0[...], (0, 0)) + dot(x1, s1[...], (0, 0))
            last = dot(a0, g0[...].reshape(tokens, width), (0, 0)) + dot(
                a1, g1[...].reshape(tokens, width), (0, 0)
            )
            for upper in range(2):
                rows = slice(upper * quarter, (upper + 1) * quarter)
                out[upper, :, 0 : 3 * width] = qkv[rows].astype(out.dtype)
                out[upper, :, 3 * width :] = last[rows].astype(out.dtype)

        @pl.when(step == 0)
        def _():
            emit(other)

        @pl.when(step == 1)
        def _():
            emit(own)

    def some(upper):
        return lambda i, c: (0, 2 * upper + jnp.where(i == 0, 1 - c[0], c[0]))

    def every(i, c):
        return (0, 0)

    flat = lambda a: a.reshape(tokens, a.shape[-1])
    ins = [(flat(a), (tokens, quarter), some(upper)) for a in mixed for upper in range(2)]
    ins += [(flat(a), (tokens, 3 * width), every) for a in stacked]
    ins += [(flat(a), (tokens, quarter), some(upper)) for a in attended for upper in range(2)]
    part = (groups, None, frames, size, cols, width)
    ins += [
        (grads, part, lambda i, c: (0, 0, 0, 0, 0, 0)),
        (grads, part, lambda i, c: (0, 1, 0, 0, 0, 0)),
    ]
    shape = (2, quarter, 4 * width)
    return call(
        body,
        (2,),
        ins,
        [(shape, dtype, shape, lambda i, c: (0, 0, 0)) for dtype in (BF16, F32)],
        flops=4 * tokens * width * width * 4,
        arrays=(core.reshape(1).astype(jnp.int32),),
        prefetch=1,
    )


def chip_sum(own, pair, lats, lons):
    upper, rows, width = own.shape
    each = rows // (lats * lons)
    part = width // 2

    def body(a, b, out):
        for half in range(upper):
            total = a[half] + b[half].astype(F32)
            for lon in range(lons):
                starts = [(lat * lons + lon) * each for lat in range(lats)]
                pieces = [total[at : at + each] for at in starts]
                out[lon, half] = jnp.concatenate(pieces, axis=0).astype(BF16)

    shape = (lons, upper, lats * each, width)
    spot = lambda i: (0, 0, i)
    return call(
        body,
        (2,),
        [(a, (upper, rows, part), spot) for a in (own, pair)],
        [(shape, BF16, shape[:3] + (part,), lambda i: (0, 0, 0, i))],
    )


def exchange(a, axis):
    return lax.all_to_all(a, axis, split_axis=0, concat_axis=0, tiled=True)


def on_device(frames_in, grad_out, kernel, w_qkv, w_out):
    local_frames, tile_lat, tile_lon, width = frames_in.shape
    half = math.isqrt(kernel.shape[0]) // 2
    frame_index = lax.axis_index("frame")
    core = lax.rem(frame_index, 2)
    clip_groups = lax.axis_size("frame")
    lats, lons = lax.axis_size("lat"), lax.axis_size("lon")

    top, bottom = frames_in[:, :half], frames_in[:, tile_lat - half :]
    above, below = rows_around(top, bottom)
    grouped = group_grads(grad_out, clip_groups)
    grads = exchange(grouped, "frame")
    left, right = ends((above, frames_in, below), half)
    sides = columns_around(left, right)
    mixed_inner = conv_forward(frames_in, above, below, (), kernel, clip_groups)
    inner = exchange(mixed_inner, "frame")
    mixed_outer = conv_forward(frames_in, above, below, sides, kernel, clip_groups)
    outer = exchange(mixed_outer, "frame")
    back_inner, stacked_inner, attended_inner = attend(inner, grads, 0, w_qkv, w_out)
    grad_inner = exchange(back_inner, "frame")
    back_outer, stacked_outer, attended_outer = attend(outer, grads, 1, w_qkv, w_out)
    grad_outer = exchange(back_outer, "frame")

    terms_other, terms_own = weight_terms(
        core,
        (inner, outer),
        (stacked_inner, stacked_outer),
        (attended_inner, attended_outer),
        grads,
    )
    swap = [(i, i ^ 1) for i in range(clip_groups)]
    terms_pair = lax.ppermute(terms_other, "frame", swap)
    cells = chip_sum(terms_own, terms_pair, lats, lons)
    cells = exchange(cells, "lon")

    top, bottom = edge_rows(grad_inner, grad_outer, half)
    grad_above, grad_below = rows_around(top, bottom)
    kernel_parts = tap_products(frames_in, (above, below, *sides), grad_inner, grad_outer, 56, lons)

    lon_parts = exchange(kernel_parts, "lon")
    left, right = edge_columns(grad_outer, grad_above, grad_below, half)
    grad_sides = columns_around(left, right)
    joined = join_terms(core, lon_parts.reshape(kernel_parts.shape), cells, lats)
    parts = exchange(joined, ("frame", "lat"))
    input_inner = conv_adjoint(
        grad_inner, grad_outer, grad_above, grad_below, (), kernel, grad_out, None
    )
    grad_input = conv_adjoint(
        grad_inner, grad_outer, grad_above, grad_below, grad_sides, kernel, grad_out, input_inner
    )
    part_sum = jnp.sum(parts.reshape(joined.shape).astype(F32), axis=0)
    rows = joined.shape[1] - kernel_parts.shape[1]
    kernel_sum = part_sum[rows : rows + kernel.shape[0]]
    proj_sum = part_sum[:rows].reshape(4, -1, width).swapaxes(0, 1).reshape(-1, 4 * width)

    cells = local_frames * clip_groups * tile_lat * tile_lon * lats * lons
    scale = cells ** (-0.5)
    return (grad_input, proj_sum * scale, kernel_sum * scale)


def solution(mesh):
    in_specs = (P("frame", "lat", "lon", None), P("frame", "lat", "lon", None), P(), P(), P())
    out_specs = (P("frame", "lat", "lon", None), P(("frame", "lat", "lon"), None), P())

    return jax.shard_map(
        on_device, mesh=mesh, in_specs=in_specs, out_specs=out_specs, check_vma=False
    )
```

```python
import math

import jax
import jax.numpy as jnp
from jax import lax
from jax.experimental import pallas as pl
from jax.experimental.pallas import tpu as pltpu
from jax.sharding import PartitionSpec as P


HEADS = 4
LANES = 128
EDGE = 8
F32 = jnp.float32
BF16 = jnp.bfloat16


def shift(piece, axis, step):
    count = lax.axis_size(axis)
    pairs = [(i, i + step) for i in range(count) if 0 <= i + step < count]
    return lax.ppermute(piece, axis, pairs)


def rows_around(top, bottom):
    above = shift(bottom, "lat", 1)
    below = shift(top, "lat", -1)
    return above, below


def columns_around(left, right):
    before = shift(right, "lon", 1)
    after = shift(left, "lon", -1)
    return before, after


def ends(parts, half):
    cols = parts[0].shape[2]
    left = jnp.concatenate([a[:, :, :half] for a in parts], axis=1)
    right = jnp.concatenate([a[:, :, cols - half :] for a in parts], axis=1)
    return left, right


def call(body, grid, ins, outs, scratch=(), flops=0, arrays=None, prefetch=0, grant=None):
    moved = sum(a.size * a.dtype.itemsize for a, _, _ in ins)
    moved += sum(math.prod(o[0]) * jnp.dtype(o[1]).itemsize for o in outs)
    results = pl.pallas_call(
        body,
        grid_spec=pltpu.PrefetchScalarGridSpec(
            num_scalar_prefetch=prefetch,
            grid=grid,
            in_specs=[pl.BlockSpec(block, index) for _, block, index in ins],
            out_specs=[pl.BlockSpec(block, index) for _, _, block, index in outs],
            scratch_shapes=scratch,
        ),
        out_shape=[jax.ShapeDtypeStruct(o[0], o[1]) for o in outs],
        compiler_params=pltpu.CompilerParams(vmem_limit_bytes=grant),
        cost_estimate=pl.CostEstimate(flops=flops, bytes_accessed=moved, transcendentals=0),
    )(*(arrays or ()), *[a for a, _, _ in ins])
    return results[0] if len(outs) == 1 else results


def in_vmem(body, ins, shapes, scalars=()):
    whole = pl.BlockSpec(memory_space=pltpu.VMEM)
    return pl.pallas_call(
        body,
        in_specs=[pl.BlockSpec(memory_space=pltpu.SMEM) for _ in scalars] + [whole] * len(ins),
        out_specs=[whole] * len(shapes),
        out_shape=[jax.ShapeDtypeStruct(shape, BF16) for shape in shapes],
        compiler_params=pltpu.CompilerParams(vmem_limit_bytes=4 << 20),
        cost_estimate=pl.CostEstimate(
            flops=0, bytes_accessed=4 * sum(a.size for a in ins), transcendentals=0
        ),
    )(*scalars, *ins)


INNER, OUTER = (8, 16), (0, 24)


def put(dst, y, col, value):
    for piece, at in enumerate(col):
        dst[y, at : at + 8, :] = value[8 * piece : 8 * piece + 8, :]


def fill_plain(pad, f, c, n, s, half):
    rows, cols = c.shape[1], c.shape[2]
    pad[half : half + rows, EDGE : EDGE + cols, :] = c[f].astype(F32)
    pad[0:half, EDGE : EDGE + cols, :] = n[f].astype(F32)
    pad[half + rows : rows + 2 * half, EDGE : EDGE + cols, :] = s[f].astype(F32)


def fill_sides(pad, f, w, e, half, cols):
    pad[:, EDGE - half : EDGE, :] = w[f].astype(F32)
    pad[:, EDGE + cols : EDGE + cols + half, :] = e[f].astype(F32)


def chunked_row(pad, y, inner, outer):
    put(pad, y, [EDGE + at for at in INNER], inner.astype(F32))
    put(pad, y, [EDGE + at for at in OUTER], outer.astype(F32))


def fill_chunked(pad, f, inner, outer, n, s, half):
    size = inner.shape[2]
    rows = inner.shape[0] * size
    for y in range(rows):
        at = (y // size, f, y % size)
        chunked_row(pad, half + y, inner[at], outer[at])
    for y in range(half):
        chunked_row(pad, y, n[f, y, 0:16, :], n[f, y, 16:32, :])
        chunked_row(pad, half + rows + y, s[f, y, 0:16, :], s[f, y, 16:32, :])


def each_frame(frames, step):
    lax.fori_loop(0, frames, lambda f, done: (step(f), done)[1], 0)


def conv_sums(pad, taps, rows, half, columns, flipped):
    side = 2 * half + 1
    sums = [[jnp.zeros((8, LANES), F32) for _ in columns] for _ in range(rows)]
    for col_tap in range(side):
        weights = []
        for row_tap in range(side):
            at = row_tap * side + col_tap
            if flipped:
                at = side * side - 1 - at
            weights.append(jnp.broadcast_to(taps[at : at + 1, :], (8, LANES)))
        for y in range(rows + side - 1):
            for part, col in enumerate(columns):
                first = EDGE - half + col + col_tap
                value = pad[y, first : first + 8, :]
                for row_tap in range(side):
                    if 0 <= y - row_tap < rows:
                        sums[y - row_tap][part] += weights[row_tap] * value
    return [jnp.concatenate(pair, axis=0) for pair in sums]


def wide_tap(kernel):
    return (kernel, (kernel.shape[0], LANES), lambda c: (0, c))


def tile4(a):
    return (a, a.shape[:3] + (LANES,), lambda c: (0, 0, 0, c))


def tile5(a):
    return (a, a.shape[:4] + (LANES,), lambda c: (0, 0, 0, 0, c))


def conv_scratch(rows, cols, half, taps):
    return [
        pltpu.VMEM((rows + 2 * half, cols + 2 * EDGE, LANES), F32),
        pltpu.VMEM((-(-taps // 8) * 8, LANES), F32),
    ]


def conv_forward(block, above, below, sides, kernel, groups):
    frames, rows, cols, width = block.shape
    count = kernel.shape[0]
    half = above.shape[1]
    size = rows // groups
    columns = OUTER if sides else INNER

    def body(c, n, s, *rest):
        if sides:
            w, e, k, out, pad, taps = rest
        else:
            k, out, pad, taps = rest
        taps[0:count, :] = k[...].astype(F32)

        def one(f):
            fill_plain(pad, f, c, n, s, half)
            if sides:
                fill_sides(pad, f, w, e, half, cols)
            for y, total in enumerate(conv_sums(pad, taps, rows, half, columns, False)):
                out[y // size, f, y % size] = total.astype(BF16)

        each_frame(frames, one)

    shape = (groups, frames, size, 16, width)
    return call(
        body,
        (width // LANES,),
        [tile4(a) for a in (block, above, below, *sides)] + [wide_tap(kernel)],
        [(shape, BF16) + tile5(jax.ShapeDtypeStruct(shape, BF16))[1:]],
        conv_scratch(rows, cols, half, count),
        flops=count * block.size,
    )


def conv_adjoint(inner, outer, above, below, sides, kernel, base, before):
    frames, rows, cols, width = base.shape
    count = kernel.shape[0]
    half = above.shape[1]
    columns = OUTER if sides else INNER

    def body(i, o, n, s, g, *rest):
        if sides:
            w, e, b, k, out, pad, taps = rest
        else:
            k, out, pad, taps = rest
        taps[0:count, :] = k[...].astype(F32)

        def one(f):
            fill_chunked(pad, f, i, o, n, s, half)
            if sides:
                fill_sides(pad, f, w, e, half, cols)
            for y, total in enumerate(conv_sums(pad, taps, rows, half, columns, True)):
                grads = g[f, y].astype(F32)
                grads = [grads[at : at + 8, :] for at in columns]
                total = total + jnp.concatenate(grads, axis=0)
                if sides:
                    pieces = [total[:8], b[f, y].astype(F32), total[8:]]
                    total = jnp.concatenate(pieces, axis=0)
                out[f, y] = total.astype(BF16)

        each_frame(frames, one)

    shape = base.shape if sides else (frames, rows, 16, width)
    extra = [tile4(a) for a in (*sides, before)] if sides else []
    return call(
        body,
        (width // LANES,),
        [tile5(inner), tile5(outer), tile4(above), tile4(below), tile4(base)]
        + extra
        + [wide_tap(kernel)],
        [(shape, BF16) + tile4(jax.ShapeDtypeStruct(shape, BF16))[1:]],
        conv_scratch(rows, cols, half, count),
        flops=count * base.size,
    )


def tap_products(block, pieces, inner, outer, out_rows, copies):
    frames, rows, cols, width = block.shape
    half = pieces[0].shape[1]
    side = 2 * half + 1
    size = inner.shape[2]

    def body(c, n, s, w, e, i, o, out, pad, wide, total):
        total[...] = jnp.zeros_like(total)

        def one(f):
            fill_plain(pad, f, c, n, s, half)
            fill_sides(pad, f, w, e, half, cols)
            for y in range(rows):
                at = (y // size, f, y % size)
                put(wide, y, INNER, i[at].astype(F32))
                put(wide, y, OUTER, o[at].astype(F32))
            for col in range(0, cols, 16):
                grads = [
                    [wide[y, col + 8 * part : col + 8 * part + 8, :] for part in range(2)]
                    for y in range(rows)
                ]
                for col_tap in range(side):
                    sums = [total[r * side + col_tap] for r in range(side)]
                    for y in range(rows + side - 1):
                        for part in range(2):
                            first = EDGE - half + col + 8 * part + col_tap
                            value = pad[y, first : first + 8, :]
                            for row_tap in range(side):
                                if 0 <= y - row_tap < rows:
                                    sums[row_tap] += value * grads[y - row_tap][part]
                    for r in range(side):
                        total[r * side + col_tap] = sums[r]

        each_frame(frames, one)
        terms = jnp.sum(total[...], axis=1).astype(BF16)
        for copy in range(copies):
            out[copy] = terms

    return call(
        body,
        (width // LANES,),
        [tile4(a) for a in (block, *pieces)] + [tile5(inner), tile5(outer)],
        [
            (
                (copies, out_rows, width),
                BF16,
                (copies, out_rows, LANES),
                lambda c: (0, 0, c),
            )
        ],
        [
            pltpu.VMEM((rows + 2 * half, cols + 2 * EDGE, LANES), F32),
            pltpu.VMEM((rows, cols, LANES), F32),
            pltpu.VMEM((out_rows, 8, LANES), F32),
        ],
        flops=2 * side * side * block.size,
    )


def group_grads(grads, groups):
    frames, rows, _, width = grads.shape
    size = rows // groups

    def body(g, out):
        for y in range(rows):
            for f in range(frames):
                x = g[f, y]
                out[y // size, 0, f, y % size] = x[8:24, :]
                out[y // size, 1, f, y % size] = jnp.concatenate([x[:8, :], x[24:, :]], axis=0)

    shape = (groups, 2, frames, size, 16, width)
    return in_vmem(body, [grads], [shape])[0]


def edge_rows(inner, outer, half):
    groups, frames, size, _, width = inner.shape
    rows = groups * size
    shape = (frames, half, 32, width)

    def body(i, o, top, bottom):
        for k in range(half):
            for out, y in ((top, k), (bottom, rows - half + k)):
                for f in range(frames):
                    at = (y // size, f, y % size)
                    out[f, k, 0:16, :] = i[at]
                    out[f, k, 16:32, :] = o[at]

    return in_vmem(body, [inner, outer], [shape, shape])


def edge_columns(outer, above, below, half):
    groups, frames, size, _, width = outer.shape
    rows = groups * size
    shape = (frames, rows + 2 * half, half, width)

    def body(o, n, s, left, right):
        for y in range(rows + 2 * half):
            for f in range(frames):
                if y < half:
                    line = n[f, y, 16:32, :]
                elif y < half + rows:
                    line = o[(y - half) // size, f, (y - half) % size]
                else:
                    line = s[f, y - half - rows, 16:32, :]
                left[f, y] = line[:half]
                right[f, y] = line[16 - half :]

    return in_vmem(body, [outer, above, below], [shape, shape])


def join_terms(core, parts, cells, lats):
    count, rows, width = parts.shape
    senders, upper, lines, _ = cells.shape
    each = lines // lats
    first = 4 * each

    def body(own, p, c, out):
        total = p[0].astype(F32)
        for i in range(1, count):
            total = total + p[i].astype(F32)
        total = total.astype(BF16)
        for half in range(upper):
            terms = c[0, half].astype(F32)
            for i in range(1, senders):
                terms = terms + c[i, half].astype(F32)
            for lat in range(lats):
                lines = terms[lat * each : (lat + 1) * each]
                lines = [lines[:, q * width : (q + 1) * width] for q in range(4)]
                lines = jnp.concatenate(lines, axis=0)
                for parity in range(2):
                    at = (2 * half + parity) * lats + lat
                    kept = jnp.where(own[0] == parity, lines, 0.0)
                    out[at, 0:first, :] = kept.astype(BF16)
                    out[at, first : first + rows, :] = total

    shape = (2 * upper * lats, first + rows, width)
    scalars = [core.reshape(1).astype(jnp.int32)]
    return in_vmem(body, [parts, cells], [shape], scalars)[0]


def dot(a, b, over):
    return lax.dot_general(a, b, ((over[:1], over[1:]), ((), ())), preferred_element_type=F32)


def attend_body(x, g, w_qkv, w_out, token_grad, stacked, attended):
    groups, frames, size, cells, width = x.shape
    rows = groups * frames * cells
    depth = width // HEADS
    scale = depth ** (-0.5)

    def lines(ref):
        return jnp.concatenate([ref[:, :, y].reshape(rows, width) for y in range(size)], axis=0)

    def keep(ref, value):
        for y in range(size):
            part = value[y * rows : (y + 1) * rows]
            ref[:, :, y] = part.reshape(groups, frames, cells, value.shape[1])

    all_projected = dot(lines(x), w_qkv[...], (1, 0)).astype(BF16)
    all_grad_att = dot(lines(g), w_out[...], (1, 1)).astype(BF16)
    at_row = lax.broadcasted_iota(jnp.int32, (rows, rows), 0)
    at_col = lax.broadcasted_iota(jnp.int32, (rows, rows), 1)
    same = lax.rem(at_row, cells) == lax.rem(at_col, cells)
    attended_rows, grad_rows = [], []
    for y in range(size):
        projected = all_projected[y * rows : (y + 1) * rows]
        grad_att = all_grad_att[y * rows : (y + 1) * rows]
        attended_parts, query_parts, key_parts, value_parts = [], [], [], []
        for head in range(HEADS):
            at = head * depth
            query = projected[:, at : at + depth]
            key = projected[:, width + at : width + at + depth]
            value = projected[:, 2 * width + at : 2 * width + at + depth]
            grad_a = grad_att[:, at : at + depth]
            scores = dot(key, query, (1, 1)) * scale
            raised = jnp.exp(jnp.where(same, scores, -jnp.inf))
            probs = raised * (1.0 / jnp.sum(raised, axis=0, keepdims=True))
            low = probs.astype(BF16)
            attended_parts.append(dot(low, value, (0, 0)).astype(BF16))
            grad_probs = dot(value, grad_a, (1, 1))
            inner = jnp.sum(probs * grad_probs, axis=0, keepdims=True)
            grad_scores = (probs * (grad_probs - inner) * scale).astype(BF16)
            query_parts.append(dot(grad_scores, key, (0, 0)).astype(BF16))
            key_parts.append(dot(grad_scores, query, (1, 0)).astype(BF16))
            value_parts.append(dot(low, grad_a, (1, 0)).astype(BF16))
        attended_rows.append(jnp.concatenate(attended_parts, axis=1))
        grad_rows.append(jnp.concatenate(query_parts + key_parts + value_parts, axis=1))
    keep(attended, jnp.concatenate(attended_rows, axis=0))
    grad_qkv = jnp.concatenate(grad_rows, axis=0)
    keep(stacked, grad_qkv)
    keep(token_grad, dot(grad_qkv, w_qkv[...], (1, 1)).astype(BF16))


def attend(mixed, grads, chunk, w_qkv, w_out):
    groups, frames, size, cols, width = mixed.shape
    tokens = groups * frames * size * cols

    def spot(i):
        return (0, 0, 0, 0, 0)

    def rows_of(columns):
        return (groups, frames, size, cols, columns)

    def all_of(columns):
        return (groups, frames, size, cols, columns)

    return call(
        attend_body,
        (1,),
        [
            (mixed, rows_of(width), spot),
            (
                grads,
                (groups, None, frames, size, cols, width),
                lambda i: (0, chunk, 0, 0, 0, 0),
            ),
            (w_qkv, w_qkv.shape, lambda i: (0, 0)),
            (w_out, w_out.shape, lambda i: (0, 0)),
        ],
        [(all_of(c), BF16, rows_of(c), spot) for c in (width, 3 * width, width)],
        flops=2 * tokens * width * width * 8,
    )


def weight_terms(core, mixed, stacked, attended, grads):
    groups, frames, size, cols, width = mixed[0].shape
    tokens = groups * frames * size * cols
    quarter = width // 4

    def body(core, *refs):
        x, (s0, s1), a, (g0, g1), (other, own) = (
            refs[0:4], refs[4:6], refs[6:10], refs[10:12], refs[12:14]
        )
        step = pl.program_id(0)

        def emit(out):
            x0 = jnp.concatenate([x[0][...], x[1][...]], axis=1)
            x1 = jnp.concatenate([x[2][...], x[3][...]], axis=1)
            a0 = jnp.concatenate([a[0][...], a[1][...]], axis=1)
            a1 = jnp.concatenate([a[2][...], a[3][...]], axis=1)
            qkv = dot(x0, s0[...], (0, 0)) + dot(x1, s1[...], (0, 0))
            last = dot(a0, g0[...].reshape(tokens, width), (0, 0)) + dot(
                a1, g1[...].reshape(tokens, width), (0, 0)
            )
            for upper in range(2):
                rows = slice(upper * quarter, (upper + 1) * quarter)
                out[upper, :, 0 : 3 * width] = qkv[rows].astype(out.dtype)
                out[upper, :, 3 * width :] = last[rows].astype(out.dtype)

        @pl.when(step == 0)
        def _():
            emit(other)

        @pl.when(step == 1)
        def _():
            emit(own)

    def some(upper):
        return lambda i, c: (0, 2 * upper + jnp.where(i == 0, 1 - c[0], c[0]))

    def every(i, c):
        return (0, 0)

    flat = lambda a: a.reshape(tokens, a.shape[-1])
    ins = [(flat(a), (tokens, quarter), some(upper)) for a in mixed for upper in range(2)]
    ins += [(flat(a), (tokens, 3 * width), every) for a in stacked]
    ins += [(flat(a), (tokens, quarter), some(upper)) for a in attended for upper in range(2)]
    part = (groups, None, frames, size, cols, width)
    ins += [
        (grads, part, lambda i, c: (0, 0, 0, 0, 0, 0)),
        (grads, part, lambda i, c: (0, 1, 0, 0, 0, 0)),
    ]
    shape = (2, quarter, 4 * width)
    return call(
        body,
        (2,),
        ins,
        [(shape, dtype, shape, lambda i, c: (0, 0, 0)) for dtype in (BF16, F32)],
        flops=4 * tokens * width * width * 4,
        arrays=(core.reshape(1).astype(jnp.int32),),
        prefetch=1,
    )


def chip_sum(own, pair, lats, lons):
    upper, rows, width = own.shape
    each = rows // (lats * lons)
    part = width

    def body(a, b, out):
        for half in range(upper):
            total = a[half] + b[half].astype(F32)
            for lon in range(lons):
                starts = [(lat * lons + lon) * each for lat in range(lats)]
                pieces = [total[at : at + each] for at in starts]
                out[lon, half] = jnp.concatenate(pieces, axis=0).astype(BF16)

    shape = (lons, upper, lats * each, width)
    spot = lambda i: (0, 0, i)
    return call(
        body,
        (1,),
        [(a, (upper, rows, part), spot) for a in (own, pair)],
        [(shape, BF16, shape[:3] + (part,), lambda i: (0, 0, 0, i))],
        grant=67_043_328,
    )


def exchange(a, axis):
    return lax.all_to_all(a, axis, split_axis=0, concat_axis=0, tiled=True)


def on_device(frames_in, grad_out, kernel, w_qkv, w_out):
    local_frames, tile_lat, tile_lon, width = frames_in.shape
    half = math.isqrt(kernel.shape[0]) // 2
    frame_index = lax.axis_index("frame")
    core = lax.rem(frame_index, 2)
    clip_groups = lax.axis_size("frame")
    lats, lons = lax.axis_size("lat"), lax.axis_size("lon")

    top, bottom = frames_in[:, :half], frames_in[:, tile_lat - half :]
    above, below = rows_around(top, bottom)
    grouped = group_grads(grad_out, clip_groups)
    grads = exchange(grouped, "frame")
    left, right = ends((above, frames_in, below), half)
    sides = columns_around(left, right)
    mixed_inner = conv_forward(frames_in, above, below, (), kernel, clip_groups)
    inner = exchange(mixed_inner, "frame")
    mixed_outer = conv_forward(frames_in, above, below, sides, kernel, clip_groups)
    outer = exchange(mixed_outer, "frame")
    back_inner, stacked_inner, attended_inner = attend(inner, grads, 0, w_qkv, w_out)
    grad_inner = exchange(back_inner, "frame")
    back_outer, stacked_outer, attended_outer = attend(outer, grads, 1, w_qkv, w_out)
    grad_outer = exchange(back_outer, "frame")

    terms_other, terms_own = weight_terms(
        core,
        (inner, outer),
        (stacked_inner, stacked_outer),
        (attended_inner, attended_outer),
        grads,
    )
    swap = [(i, i ^ 1) for i in range(clip_groups)]
    terms_pair = lax.ppermute(terms_other, "frame", swap)
    cells = chip_sum(terms_own, terms_pair, lats, lons)
    cells = exchange(cells, "lon")

    top, bottom = edge_rows(grad_inner, grad_outer, half)
    grad_above, grad_below = rows_around(top, bottom)
    kernel_parts = tap_products(frames_in, (above, below, *sides), grad_inner, grad_outer, 56, lons)

    lon_parts = exchange(kernel_parts, "lon")
    left, right = edge_columns(grad_outer, grad_above, grad_below, half)
    grad_sides = columns_around(left, right)
    joined = join_terms(core, lon_parts.reshape(kernel_parts.shape), cells, lats)
    parts = exchange(joined, ("frame", "lat"))
    input_inner = conv_adjoint(
        grad_inner, grad_outer, grad_above, grad_below, (), kernel, grad_out, None
    )
    grad_input = conv_adjoint(
        grad_inner, grad_outer, grad_above, grad_below, grad_sides, kernel, grad_out, input_inner
    )
    part_sum = jnp.sum(parts.reshape(joined.shape).astype(F32), axis=0)
    rows = joined.shape[1] - kernel_parts.shape[1]
    kernel_sum = part_sum[rows : rows + kernel.shape[0]]
    proj_sum = part_sum[:rows].reshape(4, -1, width).swapaxes(0, 1).reshape(-1, 4 * width)

    cells = local_frames * clip_groups * tile_lat * tile_lon * lats * lons
    scale = cells ** (-0.5)
    return (grad_input, proj_sum * scale, kernel_sum * scale)


def solution(mesh):
    in_specs = (P("frame", "lat", "lon", None), P("frame", "lat", "lon", None), P(), P(), P())
    out_specs = (P("frame", "lat", "lon", None), P(("frame", "lat", "lon"), None), P())

    return jax.shard_map(
        on_device, mesh=mesh, in_specs=in_specs, out_specs=out_specs, check_vma=False
    )
```
